32 devices in a mesh: dp: 8 (over y, x, core), tensor: 4 (over z).
Axes of the slice: x: 2, y: 2, z: 4, core: 2. Of those that a mesh axis runs over, the one named last changes fastest.
Arguments:
- inputs: bfloat16 [32, 512, 768], P('dp'), may hold values from -6 to 6
- lengths: int32 [32], P('dp'), may hold values from 64 to 512, as said below
- w_query: bfloat16 [768, 768], P('dp', 'tensor'), may hold values from -0.21875 to 0.21875
- w_key: bfloat16 [768, 768], P('dp', 'tensor'), may hold values from -0.21875 to 0.21875
- w_value: bfloat16 [768, 768], P('dp', 'tensor'), may hold values from -0.21875 to 0.21875
- query_bias: float32 [768], P('tensor'), may hold values from -3 to 3
- value_bias: float32 [768], P('tensor'), may hold values from -3 to 3
- w_out: bfloat16 [768, 768], P('tensor', 'dp'), may hold values from -1.75 to 1.75
- out_bias: float32 [768], replicated, may hold values from -2 to 2
- norm1_gain: float32 [768], replicated, may hold values from 0.1 to 1.9
- norm1_shift: float32 [768], replicated, may hold values from -2 to 2
- w_inner: bfloat16 [768, 3072], P('dp', 'tensor'), may hold values from -0.21875 to 0.21875
- inner_bias: float32 [3072], P('tensor'), may hold values from -3 to 3
- w_outer: bfloat16 [3072, 768], P('tensor', 'dp'), may hold values from -0.109375 to 0.109375
- outer_bias: float32 [768], replicated, may hold values from -2 to 2
- norm2_gain: float32 [768], replicated, may hold values from 0.1 to 1.9
- norm2_shift: float32 [768], replicated, may hold values from -2 to 2
- cotangent: bfloat16 [32, 512, 768], P('dp', 'tensor'), may hold values from -6 to 6
Outputs:
- layer_out: bfloat16 [32, 512, 768], P('dp', 'tensor')
- input_grad: float32 [32, 512, 768], P('dp', 'tensor')
- w_query_grad: float32 [768, 768], P('dp', 'tensor')
- w_key_grad: float32 [768, 768], P('dp', 'tensor')
- w_value_grad: float32 [768, 768], P('dp', 'tensor')
- query_bias_grad: float32 [768], P('tensor')
- value_bias_grad: float32 [768], P('tensor')
- w_out_grad: float32 [768, 768], P('tensor', 'dp')
- out_bias_grad: float32 [768], replicated
- norm1_gain_grad: float32 [768], replicated
- norm1_shift_grad: float32 [768], replicated
- w_inner_grad: float32 [768, 3072], P('dp', 'tensor')
- inner_bias_grad: float32 [3072], P('tensor')
- w_outer_grad: float32 [3072, 768], P('tensor', 'dp')
- outer_bias_grad: float32 [768], replicated
- norm2_gain_grad: float32 [768], replicated
- norm2_shift_grad: float32 [768], replicated
The draws below stay inside these ranges and needn't reach their ends.
Inputs may be any that keep to these rules, and one draw needn't show every extreme that they name: Tokens at positions lengths[s] and later of sequence s are padding and are masked as keys; some sequence has all 512 tokens valid.
All inputs are finite; a program needn't handle non-finite values.
Results may differ from the reference program's by a relative error of at most 0.018.
Values may be sent and summed in bfloat16 or wider, within the bound.
A program may use at most 192 MiB of HBM per device.

```python
import jax
import jax.numpy as jnp
from jax import lax

D = 768
HEADS = 12
HEAD = 64
FF = 3072
SEQ = 512
SEQS = 32


def draw_lengths(key, part):
    first_key, second_key = jax.random.split(jax.random.fold_in(key, 17))
    drawn = jax.random.randint(first_key, (SEQS,), SEQ // 8, SEQ + 1)
    full_slot = jax.random.randint(second_key, (), 0, SEQS)
    return jnp.where(jnp.arange(SEQS) == full_slot, SEQ, drawn).astype(jnp.int32)


def strengthened(array, key, source, target, blocks, factor):
    def block_of(axis_at):
        return (jnp.arange(array.shape[axis_at]) // (array.shape[axis_at] // blocks)).reshape((-1,) + (1,) * (array.ndim - 1 - axis_at))

    near = jax.random.permutation(key, blocks)[block_of(target)]
    other_side = (block_of(target) + blocks // 2) % blocks
    return jnp.where((block_of(source) == near) | (block_of(source) == other_side), factor * array, array)


def shard_levels(rng, dims, cuts, least, largest):
    loudness = 1.0
    for position, parts in cuts:
        heights = jax.random.uniform(jax.random.fold_in(jax.random.fold_in(rng, 6), position), (parts,), jnp.float32, least / len(cuts), largest / len(cuts))
        loudness = loudness * jnp.repeat(jnp.exp(heights), dims[position] // parts).reshape((-1,) + (1,) * (len(dims) - 1 - position))
    return loudness


def bell_draw(stream_key, extent, spread, bound, cuts=(), dtype=jnp.bfloat16):
    factor_of = shard_levels(stream_key, extent, cuts, -0.22, 0.18) if cuts else 1.0
    entries = jax.random.normal(stream_key, extent, jnp.float32) * spread * factor_of
    return jnp.minimum(jnp.maximum(entries, -bound), bound).astype(dtype)


def noise_with(key, extent, deviation, reach, cuts, heavy, held_as=jnp.bfloat16):
    result = deviation * jax.random.normal(key, extent, jnp.float32)
    if cuts:
        result = result * shard_levels(key, extent, cuts, -0.22, 0.18)
    return jnp.clip(strengthened(result, jax.random.fold_in(key, 3), *heavy), -reach, reach).astype(held_as)


def setup_inputs(seed: int = 0) -> dict:
    key_list = jax.random.split(jax.random.key(seed), 19)
    return {
        "inputs": noise_with(key_list[0], (SEQS, SEQ, D), 1.0, 6.0, ((0, 8),), (0, 2, 8, 2.0)),
        "lengths": draw_lengths(jax.random.fold_in(key_list[18], 71), 0),
        "w_query": bell_draw(key_list[2], (D, D), D ** -0.5, 0.21875, ((0, 8), (1, 4))),
        "w_key": bell_draw(key_list[3], (D, D), D ** -0.5, 0.21875, ((0, 8), (1, 4))),
        "w_value": bell_draw(key_list[4], (D, D), D ** -0.5, 0.21875, ((0, 8), (1, 4))),
        "query_bias": bell_draw(key_list[5], (D,), 0.5, 3.0, ((0, 4),), jnp.float32),
        "value_bias": bell_draw(key_list[6], (D,), 0.5, 3.0, ((0, 4),), jnp.float32),
        "w_out": bell_draw(key_list[7], (D, D), (max(1, D * 8 // SEQ)) ** -0.5, 1.75, ((0, 4), (1, 8))),
        "out_bias": bell_draw(key_list[8], (D,), 0.3, 2.0, (), jnp.float32),
        "norm1_gain": jnp.clip(1.0 + 0.18 * jax.random.normal(key_list[9], (D,), jnp.float32), 0.1, 1.9),
        "norm1_shift": bell_draw(key_list[10], (D,), 0.3, 2.0, (), jnp.float32),
        "w_inner": bell_draw(key_list[11], (D, FF), D ** -0.5, 0.21875, ((0, 8), (1, 4))),
        "inner_bias": bell_draw(key_list[12], (FF,), 0.5, 3.0, ((0, 4),), jnp.float32),
        "w_outer": bell_draw(key_list[13], (FF, D), FF ** -0.5, 0.109375, ((0, 4), (1, 8))),
        "outer_bias": bell_draw(key_list[14], (D,), 0.3, 2.0, (), jnp.float32),
        "norm2_gain": jnp.clip(1.0 + 0.18 * jax.random.normal(key_list[15], (D,), jnp.float32), 0.1, 1.9),
        "norm2_shift": bell_draw(key_list[16], (D,), 0.3, 2.0, (), jnp.float32),
        "cotangent": bell_draw(key_list[17], (SEQS, SEQ, D), 1.0, 6.0, ((0, 8), (1, 4))),
    }


highest = lax.Precision.HIGHEST

@jax.custom_vjp
def low(v):
    return lax.optimization_barrier(v.astype(jnp.bfloat16)).astype(jnp.float32)

@jax.custom_vjp
def low_back(v):
    return v

def low_keep(v):
    return (low(v), None)

def low_pass(kept, grad):
    return (grad,)

def back_keep(v):
    return (v, None)

def back_low(kept, grad):
    return (low(grad),)
low.defvjp(low_keep, low_pass)
low_back.defvjp(back_keep, back_low)

def matmul(left, right):
    return jnp.dot(left, right, precision=highest)

def normalize(residual, gain_vec, shift_vec):
    centred = residual - lax.optimization_barrier(jnp.mean(residual, axis=-1, keepdims=True))
    variance = lax.optimization_barrier(jnp.mean(centred * centred, axis=-1, keepdims=True))
    return centred * lax.rsqrt(variance + 1e-06) * gain_vec + shift_vec

def attend(queries, keys_in, values_in, length):
    block_rows = min(512, SEQ)
    key_heads = keys_in.reshape(SEQ, HEADS, HEAD)
    value_heads = values_in.reshape(SEQ, HEADS, HEAD)
    valid_keys = (jnp.arange(SEQ) < length)[None, None, :]

    def one_block(query_block):
        scores = low_back(jnp.einsum('qhd,khd->hqk', query_block, key_heads, precision=highest) * HEAD ** (-0.5))
        scores = jnp.where(valid_keys, scores, -1000000000.0)
        expons = jnp.exp(scores - lax.optimization_barrier(jnp.max(scores, axis=-1, keepdims=True)))
        softmax_rows = expons / lax.optimization_barrier(jnp.sum(expons, axis=-1, keepdims=True))
        return jnp.einsum('hqk,khd->qhd', low(softmax_rows), value_heads, precision=highest)
    blocks = lax.map(jax.checkpoint(one_block), queries.reshape(SEQ // block_rows, block_rows, HEADS, HEAD))
    return blocks.reshape(SEQ, HEADS * HEAD)

def sequence(params, seq_in, length):
    w_query, w_key, w_value, query_bias, value_bias, w_out, out_bias, norm1_gain, norm1_shift, w_inner, inner_bias, w_outer, outer_bias, norm2_gain, norm2_shift = params
    queries = low(low_back(matmul(seq_in, w_query)) + query_bias)
    keys_in = low(low_back(matmul(seq_in, w_key)))
    values_in = low(low_back(matmul(seq_in, w_value)) + value_bias)
    attended = low_back(low(attend(queries, keys_in, values_in, length)))
    residual1 = seq_in + low_back(matmul(attended, w_out)) + out_bias
    normed1 = normalize(residual1, norm1_gain, norm1_shift)
    inner = low_back(matmul(low(normed1), w_inner)) + inner_bias
    activated = low(jax.nn.gelu(inner, approximate=False))
    residual2 = normed1 + low_back(matmul(activated, w_outer)) + outer_bias
    return normalize(residual2, norm2_gain, norm2_shift)

def reference(inputs, lengths, w_query, w_key, w_value, query_bias, value_bias, w_out, out_bias, norm1_gain, norm1_shift, w_inner, inner_bias, w_outer, outer_bias, norm2_gain, norm2_shift, cotangent):
    params = tuple((param.astype(jnp.float32) for param in (w_query, w_key, w_value, query_bias, value_bias, w_out, out_bias, norm1_gain, norm1_shift, w_inner, inner_bias, w_outer, outer_bias, norm2_gain, norm2_shift)))
    zero_grads = jax.tree.map(jnp.zeros_like, params)

    def scan_step(grad_totals, scan_item):
        seq_in, length, upstream = scan_item
        out_rows, pullback = jax.vjp(lambda weights, rows: sequence(weights, rows, length), params, seq_in)
        param_grads, input_part = pullback(upstream)
        grad_totals = jax.tree.map(lambda earlier, later: earlier + later, grad_totals, param_grads)
        return (grad_totals, (out_rows.astype(jnp.bfloat16), input_part))
    grad_totals, (out_all, input_all) = lax.scan(scan_step, zero_grads, (inputs.astype(jnp.float32), lengths, cotangent.astype(jnp.float32)))
    return (out_all, input_all, grad_totals[0], grad_totals[1], grad_totals[2], grad_totals[3], grad_totals[4], grad_totals[5], grad_totals[6], grad_totals[7], grad_totals[8], grad_totals[9], grad_totals[10], grad_totals[11], grad_totals[12], grad_totals[13], grad_totals[14])
```

```python
from functools import partial
import jax, jax.numpy as jnp
from jax import lax
from jax.experimental import pallas as pl
from jax.experimental.pallas import tpu as pltpu
from jax.sharding import PartitionSpec as P

D = 768
HEAD = 64
FF = 3072
SPLIT = 2
BF = jnp.bfloat16
F32 = jnp.float32


def flip(index, bit):
    return index + bit * (1 - 2 * ((index // bit) % 2))


class Place:
    def __init__(self, dp, tp):
        self.dp, self.tp = dp, tp
        self.d = lax.axis_index("dp")
        self.t = lax.axis_index("tensor")
        self.c = self.d % 2
        count = dp.bit_length() - 1
        links = [1 << k for k in range(1, count)]
        half = len(links) // 2
        self.order0 = links
        self.order1 = links[half:] + links[:half]
        self.hops = len(links)
        self.links = links

    def mix(self, zero, one):
        return zero * (1 - self.c) + one * self.c

    def across(self, hop):
        return self.mix(flip(self.d, self.order0[hop]), flip(self.d, self.order1[hop]))

    def subset(self, hop, j, crossed):
        zero, one = self.d, self.d
        if crossed:
            zero, one = flip(zero, self.order0[hop]), flip(one, self.order1[hop])
        for k in range(hop):
            if (j >> k) & 1:
                zero, one = flip(zero, self.order0[k]), flip(one, self.order1[k])
        return self.mix(zero, one)

    def at(self, d=None, t=None):
        return {"dp": self.d if d is None else d, "tensor": self.t if t is None else t}

    def barrier(self):
        sem = pltpu.get_barrier_semaphore()
        count = 0
        for k in range(1, self.tp):
            pl.semaphore_signal(sem, 1, device_id=self.at(t=(self.t + k) % self.tp), device_id_type=pl.DeviceIdType.MESH)
            count += 1
        for bit in [1] + self.links:
            pl.semaphore_signal(sem, 1, device_id=self.at(d=flip(self.d, bit)), device_id_type=pl.DeviceIdType.MESH)
            count += 1
        pl.semaphore_wait(sem, count)


def send(src, dst, ssem, rsem, device):
    copy = pltpu.make_async_remote_copy(src_ref=src, dst_ref=dst, send_sem=ssem, recv_sem=rsem, device_id=device, device_id_type=pl.DeviceIdType.MESH)
    copy.start()
    return copy

def gather_kernel(dp, tp, shard, cot, full, cotf, lsem, zs, zr, hs, hr, cs, cr, us, ur):
    at = Place(dp, tp)
    pieces, rows, lanes = shard.shape
    share = cot.shape[1]
    at.barrier()
    def block(p, b):
        return full.at[p, pl.ds(pl.multiple_of(b * rows, rows), rows)]
    def own(p):
        return full.at[p, pl.ds(pl.multiple_of(at.d * rows, rows), rows), pl.ds(pl.multiple_of(at.t * lanes, lanes), lanes)]
    local, zc = [], []
    for p in range(pieces):
        cp = pltpu.make_async_copy(shard.at[p], own(p), lsem.at[p]); cp.start(); local.append(cp)
        zc.append([send(shard.at[p], own(p), zs.at[p, k-1], zr.at[p, k-1], at.at(t=(at.t + k) % tp)) for k in range(1, tp)])
    cotrows = cotf.at[pl.ds(pl.multiple_of(at.t * share, share), share)]
    uc = [send(cot.at[(at.t + k) % tp], cotrows, us.at[k-1], ur.at[k-1], at.at(t=(at.t + k) % tp)) for k in range(1, tp)]
    cpu = pltpu.make_async_copy(cot.at[at.t], cotrows, lsem.at[pieces]); cpu.start()
    hops = at.hops
    hc = [[None] * hops for _ in range(pieces)]
    cc = [[] for _ in range(pieces)]
    def to_core(p, b, n):
        cc[p].append(send(block(p, b), block(p, b), cs.at[p, n], cr.at[p, n], at.at(d=flip(at.d, 1))))
    def stage_at(p, stage):
        if stage == 0:
            local[p].wait()
            for c in zc[p]: c.wait_recv()
            fresh = [at.d]
        else:
            for c in hc[p][stage-1]: c.wait_recv()
            fresh = [at.subset(stage-1, j, True) for j in range(1 << (stage-1))]
        if stage < hops:
            hc[p][stage] = [send(block(p, at.subset(stage, j, False)), block(p, at.subset(stage, j, False)),
                hs.at[p, (1 << stage) - 1 + j], hr.at[p, (1 << stage) - 1 + j], at.at(d=at.across(stage))) for j in range(1 << stage)]
        for n, b in enumerate(fresh):
            to_core(p, b, (0 if stage == 0 else (1 << (stage-1))) + n)
    for step in range(pieces + hops):
        for stage in range(hops + 1):
            p = step - stage
            if 0 <= p < pieces: stage_at(p, stage)
    for p in range(pieces):
        for c in cc[p]: c.wait_recv()
    cpu.wait()
    for c in uc: c.wait()
    for p in range(pieces):
        for c in zc[p] + cc[p] + sum(hc[p], []): c.wait_send()

def gather(dp, tp, shard, cot):
    pieces, rows, lanes = shard.shape
    V = pl.BlockSpec(memory_space=pltpu.VMEM)
    dma = pltpu.SemaphoreType.DMA
    blocks = dp // 2
    return pl.pallas_call(
        partial(gather_kernel, dp, tp),
        out_shape=(jax.ShapeDtypeStruct((pieces, D, tp * lanes), BF), jax.ShapeDtypeStruct((tp * cot.shape[1], D), BF)),
        in_specs=[V, V], out_specs=(V, V),
        scratch_shapes=[dma((pieces + 1,)), dma((pieces, tp - 1)), dma((pieces, tp - 1)), dma((pieces, blocks - 1)), dma((pieces, blocks - 1)),
            dma((pieces, blocks)), dma((pieces, blocks)), dma((tp - 1,)), dma((tp - 1,))],
        compiler_params=pltpu.CompilerParams(collective_id=0, has_side_effects=True, vmem_limit_bytes=60 * 2**20),
        name="gather",
    )(shard, cot)

def scatter_kernel(dp, tp, grads, vec, out, vout, rc, rh, rz, rv, cs, cr, hs, hr, zs, zr, vs, vr):
    at = Place(dp, tp)
    pieces, rows, lanes = out.shape
    at.barrier()
    hops = at.hops
    blocks = dp // 2
    def block(p, b):
        return grads.at[p, pl.ds(pl.multiple_of(b * rows, rows), rows)]
    part = flip(at.d, 1)
    cc, hc, zc = {}, {}, {}
    def st_core(p):
        cc[p] = []
        for j in range(blocks):
            b = 2 * j + (1 - at.c)
            cc[p].append(send(block(p, b), rc.at[p, j], cs.at[p, j], cr.at[p, j], at.at(d=part)))
    def st_hop(p, stage):
        if stage == hops - 1:
            for c in cc[p]: c.wait_recv()
            for j in range(blocks):
                r = block(p, 2 * j + at.c)
                r[...] = (r[...].astype(F32) + rc[p, j].astype(F32)).astype(BF)
        else:
            st_add(p, stage + 1)
        n = 1 << stage
        hc[p, stage] = [send(block(p, at.subset(stage, j, True)), rh.at[p, n - 1 + j], hs.at[p, n - 1 + j], hr.at[p, n - 1 + j], at.at(d=at.across(stage))) for j in range(n)]
    def st_add(p, stage):
        n = 1 << stage
        for c in hc[p, stage]: c.wait_recv()
        for j in range(n):
            r = block(p, at.subset(stage, j, False))
            r[...] = (r[...].astype(F32) + rh[p, n - 1 + j].astype(F32)).astype(BF)
    def cols(p, t):
        return grads.at[p, pl.ds(pl.multiple_of(at.d * rows, rows), rows), pl.ds(pl.multiple_of(t * lanes, lanes), lanes)]
    def st_z(p):
        st_add(p, 0)
        zc[p] = [send(cols(p, (at.t + k) % tp), rz.at[p, k-1], zs.at[p, k-1], zr.at[p, k-1], at.at(t=(at.t + k) % tp)) for k in range(1, tp)]
    def st_out(p):
        total = cols(p, at.t)[...].astype(F32)
        for k in range(1, tp):
            zc[p][k-1].wait_recv()
            total += rz[p, k-1].astype(F32)
        out[p] = total
    stages = [st_core] + [partial(lambda s, p: st_hop(p, s), s) for s in range(hops - 1, -1, -1)] + [st_z, st_out]
    vout[...] = vec[...]
    vsteps = [1] + at.links
    vc = []
    def v_start(i):
        vc.append(send(vout, rv.at[i], vs.at[i], vr.at[i], at.at(d=flip(at.d, vsteps[i]))))
    for step in range(pieces + len(stages)):
        for s in range(len(stages) - 1, -1, -1):
            p = step - s
            if 0 <= p < pieces: stages[s](p)
    for i, bit in enumerate(vsteps):
        c = send(vout, rv.at[i], vs.at[i], vr.at[i], at.at(d=flip(at.d, bit)))
        c.wait()
        vout[...] = vout[...] + rv[i]
    base = len(vsteps)
    cps = [send(vout, rv.at[base + at.t], vs.at[base + k - 1], vr.at[base + k - 1], at.at(t=(at.t + k) % tp)) for k in range(1, tp)]
    rv[base + at.t] = vout[...]
    for c in cps: c.wait()
    total = rv[base]
    for k in range(1, tp): total += rv[base + k]
    vout[...] = total
    for p in range(pieces):
        for c in cc[p] + zc[p]: c.wait_send()
        for s in range(hops):
            for c in hc[p, s]: c.wait_send()

def scatter(dp, tp, grads, vec):
    pieces, _, wide = grads.shape
    rows, lanes = D // dp, wide // tp
    V = pl.BlockSpec(memory_space=pltpu.VMEM)
    dma = pltpu.SemaphoreType.DMA
    blocks = dp // 2
    nv = dp.bit_length() - 1 + tp
    return pl.pallas_call(
        partial(scatter_kernel, dp, tp),
        out_shape=(jax.ShapeDtypeStruct((pieces, rows, lanes), F32), jax.ShapeDtypeStruct(vec.shape, F32)),
        in_specs=[V, V], out_specs=(V, V),
        scratch_shapes=[pltpu.VMEM((pieces, blocks, rows, wide), BF), pltpu.VMEM((pieces, blocks - 1, rows, wide), BF), pltpu.VMEM((pieces, tp - 1, rows, lanes), BF),
            pltpu.VMEM((nv,) + vec.shape, F32),
            dma((pieces, blocks)), dma((pieces, blocks)), dma((pieces, blocks - 1)), dma((pieces, blocks - 1)), dma((pieces, tp - 1)), dma((pieces, tp - 1)), dma((nv,)), dma((nv,))],
        compiler_params=pltpu.CompilerParams(collective_id=1, has_side_effects=True, vmem_limit_bytes=60 * 2**20),
        name="scatter",
    )(grads, vec)


EPS = 1e-06


def layer_norm(residual, gain, shift):
    centred = residual - jnp.mean(residual, axis=-1, keepdims=True)
    inv = lax.rsqrt(jnp.mean(centred * centred, axis=-1, keepdims=True) + EPS)
    unit = centred * inv
    return unit * gain + shift, unit, inv


def norm_back(upstream, unit, inv, gain):
    scaled = upstream * gain
    result = inv * (
        scaled
        - jnp.mean(scaled, axis=-1, keepdims=True)
        - unit * jnp.mean(scaled * unit, axis=-1, keepdims=True)
    )
    return result, jnp.sum(upstream * unit, axis=0), jnp.sum(upstream, axis=0)


def dot(a, b):
    return jnp.dot(a, b, preferred_element_type=F32)


def dot_tn(a, b):
    return lax.dot_general(a, b, (((0,), (0,)), ((), ())), preferred_element_type=F32)


def dot_nt(a, b):
    return lax.dot_general(a, b, (((1,), (1,)), ((), ())), preferred_element_type=F32)


def heads(x):
    return x.reshape(x.shape[0], -1, HEAD)


def shards(dp, tp, inputs, lengths, w_query, w_key, w_value, query_bias, value_bias, w_out, out_bias, norm1_gain, norm1_shift,
           w_inner, inner_bias, w_outer, outer_bias, norm2_gain, norm2_shift, cotangent):
    t = lax.axis_index("tensor")
    wide = w_inner.shape[1]
    half = wide // SPLIT
    mixed = jnp.concatenate([w_query, w_key, w_value, w_out.T], axis=1)
    pieces = []
    for block in (mixed, w_inner, w_outer.T):
        pieces += [block[:, k * half:(k + 1) * half] for k in range(SPLIT)]
    full, cot = gather(dp, tp, jnp.stack(pieces), cotangent)
    full = full.reshape(3, SPLIT, D, tp, half).transpose(0, 2, 3, 1, 4)
    head = w_query.shape[1]
    quad = full[0].reshape(D, tp, 4, head)
    wq, wk, wv, wo = [quad[:, :, k].reshape(D, D) for k in range(4)]
    wi, wu = full[1].reshape(D, FF), full[2].reshape(D, FF)
    biases = lax.all_gather(jnp.concatenate([query_bias, value_bias, inner_bias]), "tensor", axis=0)
    bq, bv, bi = biases[:, :head].reshape(-1), biases[:, head:2 * head].reshape(-1), biases[:, 2 * head:].reshape(-1)
    x = lax.dynamic_index_in_dim(inputs, t, 0, keepdims=False)
    length = lax.dynamic_index_in_dim(lengths, t, 0, keepdims=False)
    valid = (jnp.arange(x.shape[0]) < length)[None, None, :]
    q = (dot(x, wq) + bq).astype(BF)
    k = dot(x, wk).astype(BF)
    v = (dot(x, wv) + bv).astype(BF)
    scale = HEAD ** -0.5
    scores = jnp.einsum("qhd,khd->hqk", heads(q), heads(k), preferred_element_type=F32) * scale
    scores = jnp.where(valid, scores, -1000000000.0)
    expons = jnp.exp(scores - jnp.max(scores, axis=-1, keepdims=True))
    probs = expons / jnp.sum(expons, axis=-1, keepdims=True)
    low = probs.astype(BF)
    attended = jnp.einsum("hqk,khd->qhd", low, heads(v), preferred_element_type=F32).reshape(x.shape).astype(BF)
    normed1, unit1, inv1 = layer_norm(x.astype(F32) + dot_nt(attended, wo) + out_bias, norm1_gain, norm1_shift)
    n1 = normed1.astype(BF)
    inner = dot(n1, wi) + bi
    activated, pull = jax.vjp(partial(jax.nn.gelu, approximate=False), inner)
    act = activated.astype(BF)
    result, unit2, inv2 = layer_norm(normed1 + dot_nt(act, wu) + outer_bias, norm2_gain, norm2_shift)
    up = cot.astype(F32)
    g2, gain2, shift2 = norm_back(up, unit2, inv2, norm2_gain)
    g2l = g2.astype(BF)
    d_outer = dot_tn(g2l, act)
    gi = pull(dot(g2l, wu))[0]
    gil = gi.astype(BF)
    d_inner = dot_tn(n1, gil)
    up1 = g2 + dot_nt(gil, wi)
    g1, gain1, shift1 = norm_back(up1, unit1, inv1, norm1_gain)
    g1l = g1.astype(BF)
    d_out = dot_tn(g1l, attended)
    ga = dot(g1l, wo).astype(BF)
    gp = jnp.einsum("qhd,khd->hqk", heads(ga), heads(v), preferred_element_type=F32)
    ds = (probs * (gp - jnp.sum(probs * gp, axis=-1, keepdims=True))).astype(BF)
    dq = jnp.einsum("hqk,khd->qhd", ds, heads(k), preferred_element_type=F32).reshape(x.shape) * scale
    dk = jnp.einsum("hqk,qhd->khd", ds, heads(q), preferred_element_type=F32).reshape(x.shape) * scale
    dv = jnp.einsum("hqk,qhd->khd", low, heads(ga), preferred_element_type=F32).reshape(x.shape)
    dql, dkl, dvl = dq.astype(BF), dk.astype(BF), dv.astype(BF)
    grad_x = g1 + dot_nt(dql, wq) + dot_nt(dkl, wk) + dot_nt(dvl, wv)
    d_mixed = jnp.stack([dot_tn(x, dql).reshape(D, tp, head), dot_tn(x, dkl).reshape(D, tp, head), dot_tn(x, dvl).reshape(D, tp, head),
                         d_out.reshape(D, tp, head)], axis=2).reshape(D, FF)
    grads = jnp.stack([d_mixed, d_inner, d_outer]).astype(BF).reshape(3, D, tp, SPLIT, half).transpose(0, 3, 1, 2, 4).reshape(3 * SPLIT, D, -1)
    vec = jnp.concatenate([jnp.sum(dq, 0), jnp.sum(dv, 0), jnp.sum(g1, 0), gain1, shift1, jnp.sum(g2, 0), gain2, shift2, jnp.sum(gi, 0)])
    own, vec = scatter(dp, tp, grads, vec.reshape(-1, 128))
    own = own.reshape(3, SPLIT, -1, half).transpose(0, 2, 1, 3).reshape(3, -1, wide)
    vec = vec.reshape(-1)
    def spread(rows):
        return lax.all_to_all(rows.reshape(tp, -1, D), "tensor", split_axis=0, concat_axis=0)
    out = spread(result.astype(BF))
    out_x = spread(grad_x.astype(BF)).astype(F32)
    def mine(v):
        return lax.dynamic_slice_in_dim(v, t * (v.shape[0] // tp), v.shape[0] // tp, 0)
    vecs = [vec[k * D:(k + 1) * D] for k in range(8)] + [vec[8 * D:]]
    return (out, out_x, own[0, :, :head], own[0, :, head:2 * head], own[0, :, 2 * head:3 * head], mine(vecs[0]), mine(vecs[1]),
            own[0, :, 3 * head:].T, vecs[2], vecs[3], vecs[4], own[1], mine(vecs[8]), own[2].T, vecs[5], vecs[6], vecs[7])


def solution(mesh):
    dp, tp = mesh.shape["dp"], mesh.shape["tensor"]
    rows, cols = P("dp", "tensor"), P("tensor", "dp")
    tokens = P("dp", "tensor", None)
    tensor, whole = P("tensor"), P()
    return jax.shard_map(
        partial(shards, dp, tp),
        mesh=mesh,
        in_specs=(P("dp", None, None), P("dp"), rows, rows, rows, tensor, tensor, cols, whole, whole, whole, rows, tensor, cols,
                  whole, whole, whole, tokens),
        out_specs=(tokens, tokens, rows, rows, rows, tensor, tensor, cols, whole, whole, whole, rows, tensor, cols, whole, whole, whole),
        check_vma=False,
    )
```

```python
from functools import partial
from types import SimpleNamespace

import jax
import jax.numpy as jnp
from jax import lax
from jax.experimental import pallas as pl
from jax.experimental.pallas import tpu as pltpu
from jax.sharding import PartitionSpec as P

D = 768
HEAD = 64
FF = 3072
SPLIT = 3
SEQ = 512
BF = jnp.bfloat16
F32 = jnp.float32

ROUTES = ((0, 0, 0), (0, 0, 0), (0, 0, 0), (0, 0, 0), (0, 0, 0), (0, 0, 0), (1, 0, 0), (0, 0, 0), (1, 0, 0))
ORDER = (
    ("astart", 0), ("astart", 1), ("az1", 0), ("astart", 2), ("az1", 1), ("astart", 3), ("az2", 0), ("az1", 2), ("astart", 4), ("az2", 1),
    ("ahop", 0, 0), ("az1", 3), ("astart", 5), ("az2", 2), ("ahop", 1, 0), ("az1", 4), ("astart", 6), ("az2", 3), ("az1", 5), ("astart", 7),
    ("ahop", 2, 0), ("ahop", 0, 1), ("az2", 4), ("aready", 0), ("proj", 0), ("ahop", 3, 0), ("az1", 6), ("astart", 8), ("az2", 5), ("ahop", 4, 0),
    ("az1", 7), ("ahop", 1, 1), ("aready", 1), ("proj", 1), ("ahop", 5, 0), ("az2", 6), ("az1", 8), ("ahop", 2, 1), ("az2", 7), ("cots",),
    ("aready", 2), ("proj", 2), ("attend", 0), ("attend", 1), ("ahop", 3, 1), ("attend", 2), ("ahop", 7, 0), ("attend", 3), ("az2", 8), ("project",),
    ("ahop", 4, 1), ("norm1",), ("ahop", 5, 1), ("aready", 3), ("inner", 3), ("aready", 4), ("inner", 4), ("ahop", 6, 1), ("aready", 5), ("inner", 5),
    ("aready", 6), ("outer", 6), ("ahop", 7, 1), ("aready", 7), ("outer", 7), ("ahop", 8, 1), ("cotr",), ("aready", 8), ("outer", 8), ("norm2",),
    ("outs",), ("grad", 6), ("score", 6), ("grad", 7), ("score", 7), ("grad", 8), ("score", 8), ("shop", 6, 1), ("iback", 6), ("shop", 7, 1),
    ("iback", 7), ("shop", 8, 1), ("iback", 8), ("back", 3), ("shop", 6, 0), ("back", 4), ("back", 5), ("norm1b",), ("outg",), ("shop", 7, 0),
    ("sz", 6), ("grad", 3), ("score", 3), ("grad", 4), ("score", 4), ("grad", 5), ("score", 5), ("shop", 8, 0), ("shop", 3, 1), ("sz", 7),
    ("attback", 0), ("shop", 4, 1), ("attback", 1), ("shop", 5, 1), ("attback", 2), ("attback", 3), ("attback", 4), ("attback", 5), ("sz", 8),
    ("sz1", 6), ("attback", 6), ("attback", 7), ("shop", 3, 0), ("sz1", 7), ("attback", 8), ("attback", 9), ("attback", 10), ("attback", 11),
    ("vec", 0), ("sz1", 8), ("gx",), ("shop", 4, 0), ("sz", 3), ("sout", 6), ("sout", 7), ("gxs", 0), ("sout", 8), ("gxs", 1), ("grad", 0),
    ("vec", 1), ("score", 0), ("shop", 5, 0), ("grad", 1), ("vec", 2), ("score", 1), ("grad", 2), ("vec", 3), ("score", 2), ("shop", 0, 1), ("sz", 4),
    ("sz1", 3), ("outr",), ("sz", 5), ("shop", 1, 1), ("shop", 2, 1), ("shop", 0, 0), ("gxw", 0), ("gxs", 2), ("sz1", 4), ("sz", 0), ("shop", 1, 0),
    ("sout", 3), ("sz1", 5), ("sz", 1), ("shop", 2, 0), ("sz", 2), ("gxw", 1), ("gxw", 2), ("gxr",), ("sout", 4), ("sz1", 0), ("sout", 5), ("sz1", 1),
    ("sz1", 2), ("sout", 0), ("sout", 1), ("sout", 2), ("vout",),
)


def flip(index, bit):
    return index + bit * (1 - 2 * ((index // bit) % 2))


class Place:
    def __init__(self, dp, tp):
        self.dp, self.tp = dp, tp
        self.d = lax.axis_index("dp")
        self.t = lax.axis_index("tensor")
        self.c = self.d % 2
        count = dp.bit_length() - 1
        links = [1 << k for k in range(1, count)]
        half = len(links) // 2
        self.order0 = links
        self.order1 = links[half:] + links[:half]
        self.hops = len(links)
        self.links = links

    def mix(self, zero, one):
        return zero * (1 - self.c) + one * self.c

    def across(self, hop):
        return self.mix(flip(self.d, self.order0[hop]), flip(self.d, self.order1[hop]))

    def subset(self, hop, j, crossed):
        zero, one = self.d, self.d
        if crossed:
            zero, one = flip(zero, self.order0[hop]), flip(one, self.order1[hop])
        for k in range(hop):
            if (j >> k) & 1:
                zero, one = flip(zero, self.order0[k]), flip(one, self.order1[k])
        return self.mix(zero, one)

    def at(self, d=None, t=None):
        return {"dp": self.d if d is None else d, "tensor": self.t if t is None else t}

    def neighbours(self):
        return [self.at(t=(self.t + k) % self.tp) for k in range(1, self.tp)] + [self.at(d=flip(self.d, bit)) for bit in [1] + self.links]

    def greet(self):
        for device in self.neighbours():
            pl.semaphore_signal(pltpu.get_barrier_semaphore(), 1, device_id=device, device_id_type=pl.DeviceIdType.MESH)

    def meet(self):
        pl.semaphore_wait(pltpu.get_barrier_semaphore(), len(self.neighbours()))


EPS = 1e-06


def dot(a, b):
    return jnp.dot(a, b, preferred_element_type=F32)


def dot_nt(a, b):
    return lax.dot_general(a, b, (((1,), (1,)), ((), ())), preferred_element_type=F32)


def dot_tn(a, b):
    return lax.dot_general(a, b, (((0,), (0,)), ((), ())), preferred_element_type=F32)


def mean(v):
    return jnp.sum(v, axis=-1, keepdims=True) * (1.0 / D)


def count_loop(first, last, body):
    def run(i, carry):
        body(i)
        return carry

    lax.fori_loop(first, last, run, 0)


def span(start, size, step=None):
    return pl.ds(pl.multiple_of(start, step or size), size)


class Layer:
    def __init__(self, r, tp):
        self.r, self.tp = r, tp
        self.seq = r.x.shape[0]
        self.head = D // tp
        self.per = self.head // HEAD
        self.lanes = r.w.shape[2] // tp

    def tile(self, t, size=None):
        return pl.ds(pl.multiple_of(t * self.lanes, self.lanes), size or self.lanes)

    def prepare(self):
        r = self.r
        r.xt[...] = r.x[...].T
        zero = jnp.zeros((HEAD, self.seq), BF)
        for t in range(self.tp):
            r.attt[t, pl.ds(0, HEAD), :] = zero
            r.qkv[t, pl.ds(3 * self.head, HEAD), :] = zero

    def project_in(self, k, t):
        r = self.r
        width = self.lanes if k < 2 else 2 * HEAD
        part = dot(r.x[...], r.w[k, :, self.tile(t, width)]) + r.bias[t, :, pl.ds(k * self.lanes, width)]
        if k == 0:
            lane = lax.broadcasted_iota(jnp.int32, (1, width), 1)
            part = part * jnp.where(lane < self.head, HEAD ** -0.5, 1.0)
        rows = part.astype(BF).T
        if k < 2:
            r.qkv[t, pl.ds(k * self.lanes, width), :] = rows
        else:
            r.qkv[t, pl.ds(k * self.lanes, HEAD), :] = rows[:HEAD]

    def head_rows(self, i):
        return [pl.ds(k * self.head + i * HEAD, HEAD) for k in range(3)]

    def attend(self, t, i):
        r = self.r
        qt, kt, vt = [r.qkv[t, rows, :] for rows in self.head_rows(i)]
        scores = dot_tn(kt, qt)
        key = lax.broadcasted_iota(jnp.int32, (self.seq, 1), 0)
        scores = jnp.where(key < r.length, scores, -1000000000.0)
        expons = jnp.exp(scores - jnp.max(scores, axis=0, keepdims=True))
        inverse = 1.0 / jnp.sum(expons, axis=0, keepdims=True)
        expons = expons.astype(BF)
        h = t * self.per + i
        r.pt[h] = expons
        r.linv[h] = inverse
        r.attt[t, pl.ds(HEAD + i * HEAD, HEAD), :] = (dot(vt, expons) * inverse).astype(BF)

    def attend_all(self, t):
        for i in range(self.per):
            self.attend(t, i)

    def project_out(self):
        r = self.r

        def part(t):
            r.att[t] = r.attt[t].T
            return dot_nt(r.att[t], r.w[2, :, self.tile(t)])

        r.acc[...] = part(0)

        def body(t):
            r.acc[...] += part(t)

        count_loop(1, self.tp, body)

    def norm1(self):
        r = self.r

        def body(i):
            rows = span(i * 64, 64)
            res = r.x[rows, :].astype(F32) + r.acc[rows, :] + r.out_bias
            centred = res - mean(res)
            inv = lax.rsqrt(mean(centred * centred) + EPS)
            unit = centred * inv
            r.unit1[rows, :] = unit
            r.inv1[rows, :] = jnp.broadcast_to(inv, (inv.shape[0], 128))
            r.n1[rows, :] = (unit * r.gain1 + r.shift1).astype(BF)

        count_loop(0, self.seq // 64, body)
        r.n1t[...] = r.n1[...].T

    def inner(self, k, t):
        r = self.r
        u = dot(r.n1[...], r.w[3 + k, :, self.tile(t)]) + r.bias[t, :, pl.ds(D + k * self.lanes, self.lanes)]
        half = 0.5 + 0.5 * lax.erf(u * (2.0 ** -0.5))
        r.act[k, :, self.tile(t)] = (u * half).astype(BF)
        r.slope[k, :, self.tile(t)] = (half + u * jnp.exp(-0.5 * u * u) * (2 * jnp.pi) ** -0.5).astype(BF)

    def outer(self, k):
        r = self.r
        for n in range(D // 256):
            cols = pl.ds(n * 256, 256)
            part = dot_nt(r.act[k], r.w[6 + k, cols, :])
            if k == 0:
                r.acc[:, cols] = part
            else:
                r.acc[:, cols] += part

    def norm2(self):
        r = self.r
        r.sums[...] = jnp.zeros_like(r.sums)

        def body(i):
            rows = span(i * 64, 64)
            res = r.unit1[rows, :] * r.gain1 + r.shift1 + r.acc[rows, :] + r.outer_bias
            centred = res - mean(res)
            inv = lax.rsqrt(mean(centred * centred) + EPS)
            unit = centred * inv
            r.out[rows, :] = (unit * r.gain2 + r.shift2).astype(BF)
            grad = self.norm_back(r.cot[rows, :].astype(F32), unit, inv, r.gain2, 3)
            r.acc[rows, :] = grad
            r.g[rows, :] = grad.astype(BF)

        count_loop(0, self.seq // 64, body)
        r.gt[...] = r.g[...].T

    def norm_back(self, up, unit, inv, gain, slot):
        r = self.r
        scaled = up * gain
        grad = inv * (scaled - mean(scaled) - unit * mean(scaled * unit))

        def total(v):
            return jnp.sum(v.reshape(-1, 8, D), axis=0)

        r.sums[slot] += total(grad)
        r.sums[slot + 1] += total(up * unit)
        r.sums[slot + 2] += total(up)
        return grad

    def outer_grad(self, k, t):
        r = self.r
        r.dc[k, :, self.tile(t)] = dot(r.gt[...], r.act[k, :, self.tile(t)]).astype(BF)

    def inner_back(self, k, t):
        r = self.r
        grad = dot(r.g[...], r.w[6 + k, :, self.tile(t)]) * r.slope[k, :, self.tile(t)].astype(F32)
        r.isum[k, :, self.tile(t)] = jnp.sum(grad.reshape(-1, 8, self.lanes), axis=0)
        r.slope[k, :, self.tile(t)] = grad.astype(BF)

    def inner_grad(self, k, t):
        r = self.r
        r.w[6 + k, :, self.tile(t)] = dot(r.n1t[...], r.slope[k, :, self.tile(t)]).astype(BF)

    def back(self, k):
        r = self.r
        for n in range(D // 256):
            cols = pl.ds(n * 256, 256)
            r.acc[:, cols] += dot_nt(r.slope[k], r.w[3 + k, cols, :])

    def norm1_back(self):
        r = self.r

        def body(i):
            rows = span(i * 64, 64)
            grad = self.norm_back(r.acc[rows, :], r.unit1[rows, :], r.inv1[rows, :1], r.gain1, 0)
            r.acc[rows, :] = grad
            r.g[rows, :] = grad.astype(BF)

        count_loop(0, self.seq // 64, body)
        r.gt[...] = r.g[...].T

    def out_grad(self, t):
        r = self.r
        r.w[5, :, self.tile(t)] = dot(r.gt[...], r.att[t]).astype(BF)
        r.attt[t] = dot(r.g[...], r.w[2, :, self.tile(t)]).astype(BF).T

    def attend_back(self, t, i):
        r = self.r
        q_rows, k_rows, v_rows = self.head_rows(i)
        qt, kt, vt = r.qkv[t, q_rows, :], r.qkv[t, k_rows, :], r.qkv[t, v_rows, :]
        h = t * self.per + i
        inverse = r.linv[h]
        gat = (r.attt[t, pl.ds(HEAD + i * HEAD, HEAD), :].astype(F32) * inverse).astype(BF)
        expons = r.pt[h]
        gp = dot_tn(vt, gat)
        wide = expons.astype(F32)
        delta = jnp.sum(wide * gp, axis=0, keepdims=True) * inverse
        gs = (wide * (gp - delta)).astype(BF)
        dqt = dot(kt, gs) * HEAD ** -0.5
        dkt = dot_nt(qt, gs)
        dvt = dot_nt(gat, expons)
        r.qkv[t, q_rows, :] = dqt.astype(BF)
        r.qkv[t, k_rows, :] = dkt.astype(BF)
        r.qkv[t, v_rows, :] = dvt.astype(BF)

        def fold(v):
            return sum(v[:, n:n + 128] for n in range(128, self.seq, 128)) + v[:, :128]

        r.qsum[span(h * HEAD, HEAD), :] = fold(dqt)
        r.vsum[span(h * HEAD, HEAD), :] = fold(dvt)

    def attend_back_all(self, t):
        for i in range(self.per):
            self.attend_back(t, i)

    def mixed_grad(self, k, t):
        r = self.r
        if k < 2:
            r.w[3 + k, :, self.tile(t)] = dot_nt(r.xt[...], r.qkv[t, pl.ds(k * self.lanes, self.lanes), :]).astype(BF)
        else:
            r.w[5, :, self.tile(t, 2 * HEAD)] += dot_nt(r.xt[...], r.qkv[t, pl.ds(k * self.lanes, 2 * HEAD), :]).astype(BF)

    def input_grad(self):
        r = self.r

        def part(t, tokens):
            total = 0.0
            for k in range(3):
                width = self.lanes if k < 2 else 2 * HEAD
                total += dot(r.w[k, :, self.tile(t, width)], r.qkv[t, pl.ds(k * self.lanes, width), tokens])
            return total

        for n in range(self.seq // 256):
            tokens = pl.ds(n * 256, 256)
            r.gxt[...] = part(0, tokens)

            def body(t):
                r.gxt[...] += part(t, tokens)

            count_loop(1, self.tp, body)
            r.n1[tokens, :] = (r.gxt[...].T + r.acc[tokens, :]).astype(BF)


def layer_kernel(dp, tp, order, routes, n_in, n_out, *refs):
    names = [n for n, _ in scratch_list(dp, tp)]
    ins, outs, rest = refs[:n_in], refs[n_in:n_in + n_out], refs[n_in + n_out:]
    r = SimpleNamespace(**dict(zip(names, rest)))
    lengths, inputs, cot = ins[:3]
    local = rest[len(names):]
    wq, wk, wv, wo, wi, wu, bq, bv, bi = local[:9]
    vectors_in = local[9:]
    own_out, vec_out, layer_out, gx_out = outs
    r.g, r.out = r.cot, r.x
    at = Place(dp, tp)
    pieces, rows, lanes = r.stage.shape
    share = cot.shape[1]
    hops, blocks = at.hops, dp // 2
    half = hops // 2
    groups = [range(half), range(half, hops)]
    r.length = lengths[at.t]
    L = Layer(r, tp)
    beside, two = flip(at.t, 1), flip(at.t, 2)
    peers = (beside, two, flip(two, 1))
    partner = at.at(d=flip(at.d, 1))

    def row_block(b):
        return span(b * rows, rows)

    def columns(t, count=1):
        return pl.ds(pl.multiple_of(t * (count * lanes), lanes), count * lanes)

    def copy(src, dst, ssem, rsem, device):
        return pltpu.make_async_remote_copy(src_ref=src, dst_ref=dst, send_sem=ssem, recv_sem=rsem, device_id=device, device_id_type=pl.DeviceIdType.MESH)

    def go(copies):
        for c in copies:
            c.start()

    def received(copies):
        for c in copies:
            c.wait_recv()

    def sent(copies):
        for c in copies:
            c.wait_send()

    def done(copies):
        for c in copies:
            c.wait()

    def weight(p, b, cols=None):
        return r.w.at[p, row_block(b)] if cols is None else r.w.at[p, row_block(b), cols]

    def place_weights():
        mixed = jnp.concatenate([wq[...], wk[...], wv[...], wo[...].T], axis=1)
        outer = wu
        r.bstage[...] = jnp.zeros_like(r.bstage)
        for start, b in ((0, bq), (2 * bq.shape[0], bv), (D, bi)):
            r.bstage[0, :, start:start + b.shape[0]] = b[...].reshape(1, b.shape[0])
        for p in range(pieces):
            k = p % SPLIT
            block = (mixed, wi, outer)[p // SPLIT][:, k * lanes:(k + 1) * lanes]
            r.stage[p] = block
            r.w[p, row_block(at.d), columns(at.t)] = block

    def a_hop(p, stage):
        out = []
        for j in range(1 << stage):
            b = at.subset(stage, j, False)
            n = (1 << stage) - 1 + j
            dst = weight(p, b, columns(at.t)) if stage < routes[p][0] else weight(p, b)
            src = r.stage.at[p] if stage == 0 and routes[p][0] else dst
            out.append(copy(src, dst, r.hs.at[p, n], r.hr.at[p, n], at.at(d=at.across(stage))))
        return out

    def a_core(p, fresh, base):
        return [copy(weight(p, b), weight(p, b), r.cs.at[p, base + n], r.cr.at[p, base + n], partner) for n, b in enumerate(fresh)]

    def a_core_z(p):
        return a_core(p, [at.subset(routes[p][0], j, False) for j in range(1 << routes[p][0])], 0)

    def a_core_hop(p, stage):
        return a_core(p, [at.subset(stage, j, True) for j in range(1 << stage)], 1 << stage)

    def a_line(p, step):
        if routes[p][1]:
            moves = [(at.t, peer) for peer in peers]
        else:
            moves = ([(at.t, two)], [(at.t, beside), (two, beside)])[step]
        out = []
        for n, (t, peer) in enumerate(moves):
            for j in range(1 << routes[p][0]):
                b = at.subset(routes[p][0], j, False)
                src = r.stage.at[p] if n == 0 and step == 0 and not routes[p][0] else weight(p, b, columns(t))
                k = n if routes[p][1] else step + n
                out.append(copy(src, weight(p, b, columns(t)), r.zs.at[p, k, j], r.zr.at[p, k, j], at.at(t=peer)))
        return out

    def a_first(p):
        if routes[p][0]:
            go(a_hop(p, 0))

    def a_start(p):
        if routes[p][0]:
            for s in groups[0]:
                received(a_hop(p, s))
                if s + 1 < half:
                    go(a_hop(p, s + 1))
        go(a_line(p, 0))

    def a_z1(p):
        received(a_line(p, 0))
        go(a_line(p, 1))

    def a_z2(p):
        received(a_line(p, 0 if routes[p][1] else 1))
        if routes[p][0] < hops:
            go(a_hop(p, routes[p][0]))
        go(a_core_z(p))

    def a_group(p, g):
        for s in groups[g]:
            received(a_hop(p, s))
            if s + 1 < hops:
                go(a_hop(p, s + 1))
            go(a_core_hop(p, s))

    def a_ready(p):
        received(a_core_z(p))
        for s in range(routes[p][0], hops):
            received(a_core_hop(p, s))

    def a_sent():
        for p in range(pieces):
            for s in range(hops):
                sent(a_hop(p, s))
                if s >= routes[p][0]:
                    sent(a_core_hop(p, s))
            sent(a_core_z(p) + a_line(p, 0))
            if not routes[p][1]:
                sent(a_line(p, 1))

    where = [r.w.at[3 + k] for k in range(3)] + [r.w.at[6 + k] for k in range(3)] + [r.dc.at[k] for k in range(3)]

    def part(p, b, cols=None):
        return where[p].at[row_block(b)] if cols is None else where[p].at[row_block(b), cols]

    def add(ref, other):
        def body(i):
            s = span(i * 8, 8)
            ref[s, :] = (ref[s, :].astype(F32) + other[s, :].astype(F32)).astype(BF)

        count_loop(0, rows // 8, body)

    def s_core(p):
        return [copy(part(p, 2 * j + (1 - at.c)), r.rc.at[p, j], r.scs.at[p, j], r.scr.at[p, j], partner) for j in range(blocks)]

    def s_hop(p, stage):
        first = (1 << stage) - 1
        out = []
        for j in range(1 << stage):
            src, dst = part(p, at.subset(stage, j, True)), r.rh.at[p, first + j]
            if stage < routes[p][2]:
                src, dst = part(p, at.subset(stage, j, True), columns(at.t)), r.rh.at[p, first + j, :, pl.ds(0, lanes)]
            out.append(copy(src, dst, r.shs.at[p, first + j], r.shr.at[p, first + j], at.at(d=at.across(stage))))
        return out

    def s_added(p, stage):
        received(s_hop(p, stage))
        for j in range(1 << stage):
            b, other = at.subset(stage, j, False), r.rh.at[p, (1 << stage) - 1 + j]
            if stage < routes[p][2]:
                add(part(p, b, columns(at.t)), other.at[:, pl.ds(0, lanes)])
            else:
                add(part(p, b), other)

    def s_rest(p, g):
        for s in reversed(groups[g]):
            s_added(p, s)
            if s != groups[g][0]:
                go(s_hop(p, s - 1))

    def s_line(p, step):
        moves = ([(beside, beside), (flip(two, 1), beside)], [(two, two)])[step]
        out = []
        for n, (t, peer) in enumerate(moves):
            for j in range(1 << routes[p][2]):
                src = part(p, at.subset(routes[p][2], j, False), columns(t))
                out.append(copy(src, r.rz.at[p, 2 * step + n, j], r.szs.at[p, 2 * step + n, j], r.szr.at[p, 2 * step + n, j], at.at(t=peer)))
        return out

    def s_line_add(p, step):
        received(s_line(p, step))
        for n, t in enumerate(((at.t, two), (at.t,))[step]):
            for j in range(1 << routes[p][2]):
                add(part(p, at.subset(routes[p][2], j, False), columns(t)), r.rz.at[p, 2 * step + n, j])

    def s_group(p, g):
        if g == 1:
            received(s_core(p))
            for j in range(blocks):
                add(part(p, 2 * j + at.c), r.rc.at[p, j])
        elif routes[p][2]:
            s_line_add(p, 1)
        else:
            s_rest(p, 1)
        go(s_hop(p, groups[g][-1]))

    def s_z(p):
        s_rest(p, 1 if routes[p][2] else 0)
        go(s_line(p, 0))

    def s_z1(p):
        s_line_add(p, 0)
        go(s_line(p, 1))

    def s_out(p):
        if routes[p][2]:
            for s in reversed(range(1, half)):
                s_added(p, s)
                go(s_hop(p, s - 1))
            received(s_hop(p, 0))
            other = r.rh[p, 0, :, :lanes]
        else:
            received(s_line(p, 1))
            other = r.rz[p, 2, 0]
        r.own[p] = part(p, at.d, columns(at.t))[...].astype(F32) + other.astype(F32)
        own_move(p).start()

    def own_move(p):
        return pltpu.make_async_copy(r.own.at[p], own_out.at[p], r.osem.at[p])

    def s_sent():
        for p in range(pieces):
            sent(s_core(p) + s_line(p, 0) + s_line(p, 1))
            for s in range(hops):
                sent(s_hop(p, s))


    def token_block(t):
        return span(t * share, share)

    def exchange(n, k, src, dst):
        return copy(src(peers[k]), dst, r.us.at[n, k], r.ur.at[n, k], at.at(t=peers[k]))

    def keep(n, src, dst):
        return pltpu.make_async_copy(src(at.t), dst, r.lsem.at[n])

    def bias_move(k=None):
        args = (0, lambda t: r.bstage.at[0], r.bias.at[at.t])
        return keep(*args) if k is None else exchange(args[0], k, *args[1:])

    def cot_move(k=None):
        args = (1, lambda t: cot.at[t], r.cot.at[token_block(at.t)])
        return keep(*args) if k is None else exchange(args[0], k, *args[1:])

    def out_move(k=None):
        args = (2, lambda t: r.out.at[token_block(t)], layer_out.at[at.t])
        return keep(*args) if k is None else exchange(args[0], k, *args[1:])

    def gx_move(k=None):
        args = (3, lambda t: r.n1.at[token_block(t)], gx_out.at[at.t])
        return keep(*args) if k is None else exchange(args[0], k, *args[1:])

    every = (None, 0, 1, 2)

    links = [1] + at.links
    base = len(links)

    def v_pack():
        for k in range(6):
            r.vec[k:k + 1, :] = jnp.sum(r.sums[k], axis=0, keepdims=True)
        r.vec[6:7, :] = jnp.sum(r.qsum[...].T, axis=0, keepdims=True)
        r.vec[7:8, :] = jnp.sum(r.vsum[...].T, axis=0, keepdims=True)
        for k in range(SPLIT):
            row = jnp.sum(r.isum[k], axis=0, keepdims=True)
            for t in range(tp):
                r.vec[8 + t:9 + t, k * lanes:(k + 1) * lanes] = row[:, t * lanes:(t + 1) * lanes]
        r.vec[8 + tp:, :] = jnp.zeros((8 - tp, D), F32)

    def v_hop(i):
        return copy(r.vec, r.rv.at[i], r.vs.at[i], r.vr.at[i], at.at(d=flip(at.d, links[i])))

    def v_end(i):
        v_hop(i).wait()
        r.vec[...] = r.vec[...] + r.rv[i]

    def v_line():
        return [copy(r.vec, r.rv.at[base + at.t], r.vs.at[base + k], r.vr.at[base + k], at.at(t=peers[k])) for k in range(tp - 1)]

    def v_out():
        done(v_line())
        total = r.rv[base]
        for k in range(1, tp):
            total += r.rv[base + k]
        r.vec[...] = total
        vec_move().start()

    def vec_move():
        return pltpu.make_async_copy(r.vec, vec_out, r.osem.at[pieces])

    def each(body, first=0, last=None):
        count_loop(first, tp if last is None else last, body)

    def start():
        fetches = [pltpu.make_async_copy(src, dst, r.fsem.at[n]) for n, (src, dst) in enumerate(zip(ins[3:], local))]
        fetches.append(pltpu.make_async_copy(inputs.at[at.t], r.x, r.fsem.at[len(local)]))
        go(fetches)
        at.greet()
        done(fetches[:9])
        place_weights()
        at.meet()
        for p in range(pieces):
            a_first(p)
        go([bias_move(k) for k in every])
        done(fetches[9:])
        r.out_bias, r.gain1, r.shift1, r.outer_bias, r.gain2, r.shift2 = [v[...].reshape(1, D) for v in vectors_in]
        L.prepare()

    def project_in(k):
        if k == 0:
            done([bias_move(n) for n in every])
        each(partial(L.project_in, k))

    def vectors(i):
        if i == 0:
            v_pack()
        else:
            v_end(i - 1)
        if i < base:
            v_hop(i).start()
        else:
            go(v_line())
            r.rv[base + at.t] = r.vec[...]

    def leave():
        a_sent()
        go([out_move(k) for k in every])

    tasks = {
        "astart": a_start, "az1": a_z1, "az2": a_z2, "ahop": a_group, "aready": a_ready,
        "proj": project_in,
        "attend": lambda t: each(L.attend_all, t, t + 1),
        "project": L.project_out, "norm1": L.norm1,
        "inner": lambda p: each(partial(L.inner, p - 3)),
        "outer": lambda p: L.outer(p - 6),
        "cots": lambda: go([cot_move(k) for k in every]), "cotr": lambda: done([cot_move(k) for k in every]),
        "norm2": L.norm2, "outs": leave, "outr": lambda: done([out_move(k) for k in every]),
        "grad": lambda p: each(partial((L.mixed_grad, L.inner_grad, L.outer_grad)[p // 3], p % 3)),
        "iback": lambda p: each(partial(L.inner_back, p - 6)),
        "back": lambda p: L.back(p - 3),
        "norm1b": L.norm1_back, "outg": lambda: each(L.out_grad),
        "attback": lambda h: L.attend_back(h // L.per, h % L.per),
        "gx": L.input_grad,
        "gxs": lambda k: go([gx_move(k)] + ([gx_move()] if k == 0 else [])),
        "gxw": lambda k: gx_move(k).wait_recv(),
        "gxr": lambda: (sent([gx_move(k) for k in every[1:]]), gx_move().wait()),
        "score": lambda p: go(s_core(p)), "shop": s_group, "sz": s_z, "sz1": s_z1, "sout": s_out,
        "vec": vectors, "vout": v_out,
    }
    start()
    for name, *args in order:
        tasks[name](*args)
    s_sent()
    done([own_move(p) for p in range(pieces)])
    done([vec_move()])


def scratch_list(dp, tp):
    VM, dma = pltpu.VMEM, pltpu.SemaphoreType.DMA
    lanes, wide, seq = FF // tp // SPLIT, FF // SPLIT, SEQ
    rows, head = D // dp, D // tp
    pieces, blocks, nv, heads = 3 * SPLIT, dp // 2, dp.bit_length() - 1 + tp, D // HEAD
    most = 1 << ((dp.bit_length() - 2) // 2)
    return [
        ("w", VM((pieces, D, wide), BF)), ("dc", VM((SPLIT, D, wide), BF)), ("stage", VM((pieces, rows, lanes), BF)),
        ("x", VM((seq, D), BF)), ("xt", VM((D, seq), BF)), ("cot", VM((seq, D), BF)), ("gt", VM((D, seq), BF)), ("n1", VM((seq, D), BF)), ("n1t", VM((D, seq), BF)),
        ("bstage", VM((1, 1, 2 * D), F32)), ("bias", VM((tp, 1, 2 * D), F32)),
        ("qkv", VM((tp, 3 * head + HEAD, seq), BF)), ("attt", VM((tp, head + HEAD, seq), BF)), ("att", VM((tp, seq, head + HEAD), BF)),
        ("pt", VM((heads, seq, seq), BF)), ("linv", VM((heads, 1, seq), F32)),
        ("unit1", VM((seq, D), F32)), ("inv1", VM((seq, 128), F32)), ("acc", VM((seq, D), F32)), ("gxt", VM((D, 256), F32)),
        ("act", VM((SPLIT, seq, wide), BF)), ("slope", VM((SPLIT, seq, wide), BF)),
        ("sums", VM((6, 8, D), F32)), ("isum", VM((SPLIT, 8, wide), F32)), ("qsum", VM((D, 128), F32)), ("vsum", VM((D, 128), F32)),
        ("rc", VM((pieces, blocks, rows, wide), BF)), ("rh", VM((pieces, blocks - 1, rows, wide), BF)),
        ("rz", VM((pieces, 3, most, rows, lanes), BF)),
        ("own", VM((pieces, rows, lanes), F32)), ("vec", VM((16, D), F32)), ("rv", VM((nv, 16, D), F32)),
        ("lsem", dma((4,))), ("fsem", dma((16,))), ("osem", dma((pieces + 1,))), ("zs", dma((pieces, 3, most))), ("zr", dma((pieces, 3, most))), ("hs", dma((pieces, blocks - 1))), ("hr", dma((pieces, blocks - 1))),
        ("cs", dma((pieces, blocks))), ("cr", dma((pieces, blocks))), ("scs", dma((pieces, blocks))), ("scr", dma((pieces, blocks))),
        ("shs", dma((pieces, blocks - 1))), ("shr", dma((pieces, blocks - 1))), ("szs", dma((pieces, 3, most))), ("szr", dma((pieces, 3, most))),
        ("us", dma((4, tp - 1))), ("ur", dma((4, tp - 1))), ("vs", dma((nv,))), ("vr", dma((nv,))),
    ]


def layer_call(dp, tp, operands, share):
    A, M = pl.BlockSpec(memory_space=pl.ANY), pl.BlockSpec(memory_space=pltpu.SMEM)
    S = jax.ShapeDtypeStruct
    half = (dp.bit_length() - 2) // 2
    return pl.pallas_call(
        partial(layer_kernel, dp, tp, ORDER, [(half * a, direct, half * b) for a, direct, b in ROUTES], len(operands), 4),
        out_shape=(S((3 * SPLIT, D // dp, FF // tp // SPLIT), F32), S((16, D), F32), S((tp, share, D), BF), S((tp, share, D), BF)),
        in_specs=[M] + [A] * (len(operands) - 1),
        out_specs=(A,) * 4,
        scratch_shapes=[s for _, s in scratch_list(dp, tp)] + [pltpu.VMEM(v.shape, v.dtype) for v in operands[3:]],
        compiler_params=pltpu.CompilerParams(collective_id=0, has_side_effects=True, vmem_limit_bytes=67043328),
        name="layer",
    )(*operands)


def results_kernel(tp, own, vec, out, gx, o_out, o_gx, g_query, g_key, g_value, b_query, b_value, g_out, v_out, v_gain1, v_shift1, g_inner, b_inner,
                   g_outer, v_outer, v_gain2, v_shift2):
    t = lax.axis_index("tensor")
    head = D // tp
    o_out[...] = out[...]
    for s in range(tp):
        o_gx[s] = gx[s].astype(F32)
    mixed = jnp.concatenate([own[0], own[1], own[2]], axis=1)
    g_query[...] = mixed[:, :head]
    g_key[...] = mixed[:, head:2 * head]
    g_value[...] = mixed[:, 2 * head:3 * head]
    g_out[...] = mixed[:, 3 * head:].T
    for k in range(SPLIT):
        g_inner[:, k * 256:(k + 1) * 256] = own[3 + k]
        g_outer[:, k * 256:(k + 1) * 256] = own[6 + k]
    for ref, row in ((v_out, 0), (v_gain1, 1), (v_shift1, 2), (v_outer, 3), (v_gain2, 4), (v_shift2, 5)):
        ref[...] = vec[row:row + 1, :].reshape(D)
    for k in range(tp):
        @pl.when(t == k)
        def _():
            b_query[...] = vec[6:7, k * head:(k + 1) * head].reshape(head)
            b_value[...] = vec[7:8, k * head:(k + 1) * head].reshape(head)
            b_inner[...] = vec[8 + k:9 + k, :].reshape(D)


def shards(dp, tp, inputs, lengths, w_query, w_key, w_value, query_bias, value_bias, w_out, out_bias, norm1_gain, norm1_shift,
           w_inner, inner_bias, w_outer, outer_bias, norm2_gain, norm2_shift, cotangent):
    operands = (lengths, inputs, cotangent, w_query, w_key, w_value, w_out, w_inner, w_outer.T, query_bias, value_bias, inner_bias,
                out_bias, norm1_gain, norm1_shift, outer_bias, norm2_gain, norm2_shift)
    share = cotangent.shape[1]
    own, vec, out, grad_in = layer_call(dp, tp, operands, share)
    like = lambda v: jax.ShapeDtypeStruct(v.shape, F32)
    results = pl.pallas_call(
        partial(results_kernel, tp),
        out_shape=(
            jax.ShapeDtypeStruct(cotangent.shape, BF), like(cotangent), like(w_query), like(w_key), like(w_value), like(query_bias), like(value_bias),
            like(w_out), like(out_bias), like(norm1_gain), like(norm1_shift), like(w_inner), like(inner_bias), like(w_outer.T), like(outer_bias),
            like(norm2_gain), like(norm2_shift),
        ),
        name="results",
    )(own, vec, out, grad_in)
    return results[:13] + (results[13].T,) + results[14:]


def solution(mesh):
    dp, tp = mesh.shape["dp"], mesh.shape["tensor"]
    rows, cols = P("dp", "tensor"), P("tensor", "dp")
    tokens = P("dp", "tensor", None)
    tensor, whole = P("tensor"), P()
    return jax.shard_map(
        partial(shards, dp, tp),
        mesh=mesh,
        in_specs=(P("dp", None, None), P("dp"), rows, rows, rows, tensor, tensor, cols, whole, whole, whole, rows, tensor, cols,
                  whole, whole, whole, tokens),
        out_specs=(tokens, tokens, rows, rows, rows, tensor, tensor, cols, whole, whole, whole, rows, tensor, cols, whole, whole, whole),
        check_vma=False,
    )
```

```python
from functools import partial
from types import SimpleNamespace

import jax
import jax.numpy as jnp
from jax import lax
from jax.experimental import pallas as pl
from jax.experimental.pallas import tpu as pltpu
from jax.sharding import PartitionSpec as P

D = 768
HEAD = 64
FF = 3072
SPLIT = 3
SEQ = 512
BF = jnp.bfloat16
F32 = jnp.float32

ROUTES = ((0, 0, 0), (0, 0, 0), (0, 0, 0), (0, 0, 0), (0, 0, 0), (0, 0, 0), (1, 0, 0), (0, 0, 0), (1, 0, 0))
ORDER = (
    ("astart", 0), ("astart", 1), ("az1", 0), ("astart", 2), ("az1", 1), ("astart", 3), ("az2", 0), ("az1", 2), ("astart", 4), ("az2", 1),
    ("ahop", 0, 0), ("az1", 3), ("astart", 5), ("az2", 2), ("ahop", 1, 0), ("az1", 4), ("astart", 6), ("az2", 3), ("az1", 5), ("astart", 7),
    ("ahop", 2, 0), ("ahop", 0, 1), ("az2", 4), ("aready", 0), ("proj", 0), ("ahop", 3, 0), ("az1", 6), ("astart", 8), ("az2", 5), ("ahop", 4, 0),
    ("az1", 7), ("ahop", 1, 1), ("aready", 1), ("proj", 1), ("attend", 0), ("ahop", 5, 0), ("attend", 1), ("az2", 6), ("az1", 8), ("ahop", 2, 1),
    ("az2", 7), ("cots",), ("aready", 2), ("proj", 2), ("attend", 2), ("attend", 3), ("ahop", 3, 1), ("attend", 4), ("attend", 5), ("ahop", 7, 0),
    ("project",), ("norm1",), ("az2", 8), ("aready", 3), ("inner", 3), ("ahop", 4, 1), ("aready", 4), ("inner", 4), ("ahop", 5, 1), ("aready", 5),
    ("inner", 5), ("ahop", 6, 1), ("aready", 6), ("outer", 6), ("ahop", 7, 1), ("aready", 7), ("outer", 7), ("ahop", 8, 1), ("cotr",), ("aready", 8),
    ("outer", 8), ("norm2",), ("outs",), ("grad", 6), ("score", 6), ("grad", 7), ("score", 7), ("grad", 8), ("score", 8), ("iback", 6),
    ("shop", 6, 1), ("iback", 7), ("shop", 7, 1), ("iback", 8), ("grad", 3), ("score", 3), ("grad", 4), ("score", 4), ("grad", 5), ("score", 5),
    ("shop", 6, 0), ("shop", 8, 1), ("back", 3), ("back", 4), ("back", 5), ("norm1b",), ("outg",), ("shop", 7, 0), ("shop", 3, 1), ("sz", 6),
    ("attback", 0), ("attback", 1), ("grad", 0), ("score", 0), ("shop", 8, 0), ("shop", 4, 1), ("sz", 7), ("attback", 2), ("attback", 3), ("grad", 1),
    ("score", 1), ("attback", 4), ("shop", 3, 0), ("shop", 5, 1), ("sz1", 6), ("sz1", 7), ("sz", 8), ("attback", 5), ("vec", 0), ("grad", 2),
    ("score", 2), ("vec", 1), ("shop", 4, 0), ("shop", 0, 1), ("gx",), ("sz", 3), ("sout", 6), ("sout", 7), ("gxs", 0), ("gxs", 1), ("outr",),
    ("sz1", 8), ("sz", 4), ("shop", 5, 0), ("shop", 1, 1), ("sz1", 3), ("sz", 5), ("shop", 0, 0), ("shop", 2, 1), ("gxw", 0), ("gxs", 2), ("sz", 0),
    ("shop", 1, 0), ("sout", 8), ("sz1", 4), ("sz", 1), ("shop", 2, 0), ("vec", 2), ("sout", 3), ("sz1", 5), ("sz", 2), ("vec", 3), ("gxw", 1),
    ("gxw", 2), ("gxr",), ("sz1", 0), ("sout", 4), ("sz1", 1), ("sout", 5), ("sz1", 2), ("sout", 0), ("sout", 1), ("sout", 2), ("vout",),
)


def flip(index, bit):
    return index + bit * (1 - 2 * ((index // bit) % 2))


class Place:
    def __init__(self, dp, tp):
        self.dp, self.tp = dp, tp
        self.d = lax.axis_index("dp")
        self.t = lax.axis_index("tensor")
        self.c = self.d % 2
        count = dp.bit_length() - 1
        links = [1 << k for k in range(1, count)]
        half = len(links) // 2
        self.order0 = links
        self.order1 = links[half:] + links[:half]
        self.hops = len(links)
        self.links = links

    def mix(self, zero, one):
        return zero * (1 - self.c) + one * self.c

    def across(self, hop):
        return self.mix(flip(self.d, self.order0[hop]), flip(self.d, self.order1[hop]))

    def subset(self, hop, j, crossed):
        zero, one = self.d, self.d
        if crossed:
            zero, one = flip(zero, self.order0[hop]), flip(one, self.order1[hop])
        for k in range(hop):
            if (j >> k) & 1:
                zero, one = flip(zero, self.order0[k]), flip(one, self.order1[k])
        return self.mix(zero, one)

    def at(self, d=None, t=None):
        return {"dp": self.d if d is None else d, "tensor": self.t if t is None else t}

    def neighbours(self):
        return [self.at(t=(self.t + k) % self.tp) for k in range(1, self.tp)] + [self.at(d=flip(self.d, bit)) for bit in [1] + self.links]

    def greet(self):
        for device in self.neighbours():
            pl.semaphore_signal(pltpu.get_barrier_semaphore(), 1, device_id=device, device_id_type=pl.DeviceIdType.MESH)

    def meet(self):
        pl.semaphore_wait(pltpu.get_barrier_semaphore(), len(self.neighbours()))


EPS = 1e-06
NORM_ROWS = 256


def dot(a, b):
    return jnp.dot(a, b, preferred_element_type=F32)


def dot_nt(a, b):
    return lax.dot_general(a, b, (((1,), (1,)), ((), ())), preferred_element_type=F32)


def dot_tn(a, b):
    return lax.dot_general(a, b, (((0,), (0,)), ((), ())), preferred_element_type=F32)


def mean(v):
    return jnp.sum(v, axis=-1, keepdims=True) * (1.0 / D)


def count_loop(first, last, body):
    def run(i, carry):
        body(i)
        return carry

    lax.fori_loop(first, last, run, 0)


def span(start, size, step=None):
    return pl.ds(pl.multiple_of(start, step or size), size)


QUERY, KEY, VALUE = ((0, 3), (1, 2), (2, 1)), ((1, 0), (1, 3), (2, 2)), ((1, 1), (2, 0), (2, 3))


class Layer:
    def __init__(self, r, tp):
        self.r, self.tp = r, tp
        self.seq = r.x.shape[0]
        self.head = D // tp
        self.per = self.head // HEAD
        self.wide = r.w.shape[2]
        self.lanes = self.wide // tp

    def bias(self, k):
        return jnp.concatenate([self.r.bias[t, :, pl.ds(k * self.lanes, self.lanes)] for t in range(self.tp)], axis=1)

    def pairs(self, body):
        step = 2 * self.lanes
        count_loop(0, self.wide // step, lambda n: body(span(n * step, step)))

    def place(self, where, t):
        k, chunk = where
        return k, span(t * self.lanes + chunk * HEAD, HEAD)

    def prepare(self):
        r = self.r
        r.xt[...] = r.x[...].T
        for t in range(self.tp):
            r.qkv[0, pl.ds(t * self.lanes, self.head), :] = jnp.zeros((self.head, self.seq), BF)
            r.attt[pl.ds(t * self.lanes + self.head, HEAD), :] = jnp.zeros((HEAD, self.seq), BF)

    def project_in(self, k):
        r = self.r
        r.line[...] = self.bias(k)
        chunk = lax.broadcasted_iota(jnp.int32, (1, 2 * self.lanes), 1) % self.lanes // HEAD
        scale = jnp.where(chunk == QUERY[k][1], HEAD ** -0.5, 1.0)

        def body(cols):
            rows = ((dot(r.x[...], r.w[k, :, cols]) + r.line[:, cols]) * scale).astype(BF).T
            if k:
                r.qkv[k, cols, :] = rows
            else:
                for n in range(2):
                    start = n * self.lanes + self.head
                    r.qkv[0, span(cols.start + start, HEAD), :] = rows[start:start + HEAD]

        self.pairs(body)

    def attend(self, i, t):
        r = self.r
        qt, kt, vt = [r.qkv[self.place(kind[i], t)] for kind in (QUERY, KEY, VALUE)]
        key = lax.broadcasted_iota(jnp.int32, (self.seq, 1), 0)
        scores = jnp.where(key < r.length, dot_tn(kt, qt), -1000000000.0)
        expons = jnp.exp(scores - jnp.max(scores, axis=0, keepdims=True))
        inverse = 1.0 / jnp.sum(expons, axis=0, keepdims=True)
        expons = expons.astype(BF)
        r.pt[t * self.per + i] = expons
        r.linv[t * self.per + i] = inverse
        r.attt[self.place((0, i), t)[1], :] = (dot(vt, expons) * inverse).astype(BF)

    def project_out(self):
        r = self.r
        r.att[...] = r.attt[...].T
        for n in range(D // 256):
            cols = pl.ds(n * 256, 256)
            r.acc[:, cols] = dot_nt(r.att[...], r.w[0, cols, :])

    def norm1(self):
        r = self.r

        def body(i):
            rows = span(i * NORM_ROWS, NORM_ROWS)
            res = r.x[rows, :].astype(F32) + r.acc[rows, :] + r.out_bias
            centred = res - mean(res)
            inv = lax.rsqrt(mean(centred * centred) + EPS)
            unit = centred * inv
            r.unit1[rows, :] = unit
            r.inv1[rows, :] = jnp.broadcast_to(inv, (inv.shape[0], 128))
            r.n1[rows, :] = (unit * r.gain1 + r.shift1).astype(BF)

        count_loop(0, self.seq // NORM_ROWS, body)
        r.n1t[...] = r.n1[...].T

    def inner(self, k):
        r = self.r
        r.line[...] = self.bias(3 + k)

        def body(cols):
            u = dot(r.n1[...], r.w[3 + k, :, cols]) + r.line[:, cols]
            half = 0.5 + 0.5 * lax.erf(u * (2.0 ** -0.5))
            r.act[k, :, cols] = (u * half).astype(BF)
            r.slope[k, :, cols] = (half + u * jnp.exp(-0.5 * u * u) * (2 * jnp.pi) ** -0.5).astype(BF)

        self.pairs(body)

    def outer(self, k):
        r = self.r
        for n in range(D // 256):
            cols = pl.ds(n * 256, 256)
            part = dot_nt(r.act[k], r.w[6 + k, cols, :])
            if k == 0:
                r.acc[:, cols] = part
            else:
                r.acc[:, cols] += part

    def norm2(self):
        r = self.r
        r.sums[...] = jnp.zeros_like(r.sums)

        def body(i):
            rows = span(i * NORM_ROWS, NORM_ROWS)
            res = r.unit1[rows, :] * r.gain1 + r.shift1 + r.acc[rows, :] + r.outer_bias
            centred = res - mean(res)
            inv = lax.rsqrt(mean(centred * centred) + EPS)
            unit = centred * inv
            r.out[rows, :] = (unit * r.gain2 + r.shift2).astype(BF)
            grad = self.norm_back(r.cot[rows, :].astype(F32), unit, inv, r.gain2, 3)
            r.acc[rows, :] = grad
            r.g[rows, :] = grad.astype(BF)

        count_loop(0, self.seq // NORM_ROWS, body)
        r.gt[...] = r.g[...].T

    def norm_back(self, up, unit, inv, gain, slot):
        r = self.r
        scaled = up * gain
        grad = inv * (scaled - mean(scaled) - unit * mean(scaled * unit))

        def total(v):
            return jnp.sum(v.reshape(-1, 8, D), axis=0)

        r.sums[slot] += total(grad)
        r.sums[slot + 1] += total(up * unit)
        r.sums[slot + 2] += total(up)
        return grad

    def outer_grad(self, k):
        r = self.r
        r.dc[k] = dot(r.gt[...], r.act[k]).astype(BF)

    def inner_back(self, k):
        r = self.r

        def body(cols):
            grad = dot(r.g[...], r.w[6 + k, :, cols]) * r.slope[k, :, cols].astype(F32)
            r.isum[k, :, cols] = jnp.sum(grad.reshape(-1, 8, cols.size), axis=0)
            r.slope[k, :, cols] = grad.astype(BF)

        self.pairs(body)

    def inner_grad(self, k):
        r = self.r

        def body(cols):
            r.w[6 + k, :, cols] = dot(r.n1t[...], r.slope[k, :, cols]).astype(BF)

        self.pairs(body)

    def back(self, k):
        r = self.r
        for n in range(D // 256):
            cols = pl.ds(n * 256, 256)
            r.acc[:, cols] += dot_nt(r.slope[k], r.w[3 + k, cols, :])

    def norm1_back(self):
        r = self.r

        def body(i):
            rows = span(i * NORM_ROWS, NORM_ROWS)
            grad = self.norm_back(r.acc[rows, :], r.unit1[rows, :], r.inv1[rows, :1], r.gain1, 0)
            r.acc[rows, :] = grad
            r.g[rows, :] = grad.astype(BF)

        count_loop(0, self.seq // NORM_ROWS, body)
        r.gt[...] = r.g[...].T

    def out_back(self):
        r = self.r
        r.attt[...] = dot(r.g[...], r.w[0]).astype(BF).T

    def attend_back(self, i, ts):
        r = self.r
        loaded = []
        for t in ts:
            inverse = r.linv[t * self.per + i]
            gat = (r.attt[self.place((0, i), t)[1], :].astype(F32) * inverse).astype(BF)
            loaded.append([r.qkv[self.place(kind[i], t)] for kind in (QUERY, KEY, VALUE)] + [inverse, gat])
        found = []
        for t, (qt, kt, vt, inverse, gat) in zip(ts, loaded):
            expons = r.pt[t * self.per + i]
            gp = dot_tn(vt, gat)
            wide = expons.astype(F32)
            delta = jnp.sum(wide * gp, axis=0, keepdims=True) * inverse
            gs = (wide * (gp - delta)).astype(BF)
            found.append((dot(kt, gs) * HEAD ** -0.5, dot_nt(qt, gs), dot_nt(gat, expons)))

        def fold(v):
            return sum(v[:, n:n + 128] for n in range(128, self.seq, 128)) + v[:, :128]

        for t, grads in zip(ts, found):
            for kind, grad in zip((QUERY, KEY, VALUE), grads):
                r.qkv[self.place(kind[i], t)] = grad.astype(BF)
            rows = pl.ds((t * self.per + i) * HEAD, HEAD)
            r.qsum[rows, :] = fold(grads[0])
            r.vsum[rows, :] = fold(grads[2])

    def mixed_grad(self, k):
        r = self.r
        grad = dot_nt(r.xt[...], r.qkv[k])
        if k == 0:
            grad += dot(r.gt[...], r.att[...])
        r.w[3 + k] = grad.astype(BF)

    def input_grad(self):
        r = self.r
        for n in range(self.seq // 256):
            tokens = pl.ds(n * 256, 256)
            total = dot(r.w[0], r.qkv[0, :, tokens]) + dot(r.w[1], r.qkv[1, :, tokens]) + dot(r.w[2], r.qkv[2, :, tokens])
            r.n1[tokens, :] = (total.T + r.acc[tokens, :]).astype(BF)


def layer_kernel(dp, tp, order, routes, n_in, n_out, *refs):
    names = [n for n, _ in scratch_list(dp, tp)]
    ins, outs, rest = refs[:n_in], refs[n_in:n_in + n_out], refs[n_in + n_out:]
    r = SimpleNamespace(**dict(zip(names, rest)))
    lengths, inputs, cot = ins[:3]
    local = rest[len(names):]
    wq, wk, wv, wo, wi, wu, bq, bv, bi = local[:9]
    vectors_in = local[9:]
    own_out, vec_out, layer_out, gx_out = outs
    r.g, r.out = r.cot, r.x
    at = Place(dp, tp)
    pieces, rows, lanes = r.stage.shape
    share = cot.shape[1]
    hops, blocks = at.hops, dp // 2
    half = hops // 2
    groups = [range(half), range(half, hops)]
    r.length = lengths[at.t]
    L = Layer(r, tp)
    beside, two = flip(at.t, 1), flip(at.t, 2)
    peers = (beside, two, flip(two, 1))
    partner = at.at(d=flip(at.d, 1))

    def row_block(b):
        return span(b * rows, rows)

    def columns(t, count=1):
        return pl.ds(pl.multiple_of(t * (count * lanes), lanes), count * lanes)

    def copy(src, dst, ssem, rsem, device):
        return pltpu.make_async_remote_copy(src_ref=src, dst_ref=dst, send_sem=ssem, recv_sem=rsem, device_id=device, device_id_type=pl.DeviceIdType.MESH)

    def go(copies):
        for c in copies:
            c.start()

    def received(copies):
        for c in copies:
            c.wait_recv()

    def sent(copies):
        for c in copies:
            c.wait_send()

    def done(copies):
        for c in copies:
            c.wait()

    def weight(p, b, cols=None):
        return r.w.at[p, row_block(b)] if cols is None else r.w.at[p, row_block(b), cols]

    def place_weights():
        def cut(ref, i):
            return ref[:, i * HEAD:(i + 1) * HEAD]

        mixed = jnp.concatenate([wo[...].T, cut(wq, 0), cut(wk, 0), cut(wv, 0), cut(wq, 1), cut(wk, 1), cut(wv, 1), cut(wq, 2), cut(wk, 2), cut(wv, 2)], axis=1)
        outer = wu
        query, value = bq[...].reshape(1, -1), bv[...].reshape(1, -1)
        none = jnp.zeros((1, HEAD), F32)
        r.bstage[0, :, :D] = jnp.concatenate(
            [none] * 3 + [cut(query, 0), none, cut(value, 0), cut(query, 1), none, cut(value, 1), cut(query, 2), none, cut(value, 2)], axis=1
        )
        r.bstage[0, :, D:] = bi[...].reshape(1, -1)
        for p in range(pieces):
            k = p % SPLIT
            block = (mixed, wi, outer)[p // SPLIT][:, k * lanes:(k + 1) * lanes]
            r.stage[p] = block
            r.w[p, row_block(at.d), columns(at.t)] = block

    def a_hop(p, stage):
        out = []
        for j in range(1 << stage):
            b = at.subset(stage, j, False)
            n = (1 << stage) - 1 + j
            dst = weight(p, b, columns(at.t)) if stage < routes[p][0] else weight(p, b)
            src = r.stage.at[p] if stage == 0 and routes[p][0] else dst
            out.append(copy(src, dst, r.hs.at[p, n], r.hr.at[p, n], at.at(d=at.across(stage))))
        return out

    def a_core(p, fresh, base):
        return [copy(weight(p, b), weight(p, b), r.cs.at[p, base + n], r.cr.at[p, base + n], partner) for n, b in enumerate(fresh)]

    def a_core_z(p):
        return a_core(p, [at.subset(routes[p][0], j, False) for j in range(1 << routes[p][0])], 0)

    def a_core_hop(p, stage):
        return a_core(p, [at.subset(stage, j, True) for j in range(1 << stage)], 1 << stage)

    def a_line(p, step):
        if routes[p][1]:
            moves = [(at.t, peer) for peer in peers]
        else:
            moves = ([(at.t, two)], [(at.t, beside), (two, beside)])[step]
        out = []
        for n, (t, peer) in enumerate(moves):
            for j in range(1 << routes[p][0]):
                b = at.subset(routes[p][0], j, False)
                src = r.stage.at[p] if n == 0 and step == 0 and not routes[p][0] else weight(p, b, columns(t))
                k = n if routes[p][1] else step + n
                out.append(copy(src, weight(p, b, columns(t)), r.zs.at[p, k, j], r.zr.at[p, k, j], at.at(t=peer)))
        return out

    def a_first(p):
        if routes[p][0]:
            go(a_hop(p, 0))

    def a_start(p):
        if routes[p][0]:
            for s in groups[0]:
                received(a_hop(p, s))
                if s + 1 < half:
                    go(a_hop(p, s + 1))
        go(a_line(p, 0))

    def a_z1(p):
        received(a_line(p, 0))
        go(a_line(p, 1))

    def a_z2(p):
        received(a_line(p, 0 if routes[p][1] else 1))
        if routes[p][0] < hops:
            go(a_hop(p, routes[p][0]))
        go(a_core_z(p))

    def a_group(p, g):
        for s in groups[g]:
            received(a_hop(p, s))
            if s + 1 < hops:
                go(a_hop(p, s + 1))
            go(a_core_hop(p, s))

    def a_ready(p):
        received(a_core_z(p))
        for s in range(routes[p][0], hops):
            received(a_core_hop(p, s))

    def a_sent():
        for p in range(pieces):
            for s in range(hops):
                sent(a_hop(p, s))
                if s >= routes[p][0]:
                    sent(a_core_hop(p, s))
            sent(a_core_z(p) + a_line(p, 0))
            if not routes[p][1]:
                sent(a_line(p, 1))

    where = [r.w.at[3 + k] for k in range(3)] + [r.w.at[6 + k] for k in range(3)] + [r.dc.at[k] for k in range(3)]

    def part(p, b, cols=None):
        return where[p].at[row_block(b)] if cols is None else where[p].at[row_block(b), cols]

    def add(ref, other):
        ref[...] = ref[...] + other[...]

    def s_core(p):
        return [copy(part(p, 2 * j + (1 - at.c)), r.rc.at[p, j], r.scs.at[p, j], r.scr.at[p, j], partner) for j in range(blocks)]

    def s_hop(p, stage):
        first = (1 << stage) - 1
        out = []
        for j in range(1 << stage):
            src, dst = part(p, at.subset(stage, j, True)), r.rh.at[p, first + j]
            if stage < routes[p][2]:
                src, dst = part(p, at.subset(stage, j, True), columns(at.t)), r.rh.at[p, first + j, :, pl.ds(0, lanes)]
            out.append(copy(src, dst, r.shs.at[p, first + j], r.shr.at[p, first + j], at.at(d=at.across(stage))))
        return out

    def s_added(p, stage):
        received(s_hop(p, stage))
        for j in range(1 << stage):
            b, other = at.subset(stage, j, False), r.rh.at[p, (1 << stage) - 1 + j]
            if stage < routes[p][2]:
                add(part(p, b, columns(at.t)), other.at[:, pl.ds(0, lanes)])
            else:
                add(part(p, b), other)

    def s_rest(p, g):
        for s in reversed(groups[g]):
            s_added(p, s)
            if s != groups[g][0]:
                go(s_hop(p, s - 1))

    def s_line(p, step):
        moves = ([(beside, beside), (flip(two, 1), beside)], [(two, two)])[step]
        out = []
        for n, (t, peer) in enumerate(moves):
            for j in range(1 << routes[p][2]):
                src = part(p, at.subset(routes[p][2], j, False), columns(t))
                out.append(copy(src, r.rz.at[p, 2 * step + n, j], r.szs.at[p, 2 * step + n, j], r.szr.at[p, 2 * step + n, j], at.at(t=peer)))
        return out

    def s_line_add(p, step):
        received(s_line(p, step))
        for n, t in enumerate(((at.t, two), (at.t,))[step]):
            for j in range(1 << routes[p][2]):
                add(part(p, at.subset(routes[p][2], j, False), columns(t)), r.rz.at[p, 2 * step + n, j])

    def s_group(p, g):
        if g == 1:
            received(s_core(p))
            for j in range(blocks):
                add(part(p, 2 * j + at.c), r.rc.at[p, j])
        elif routes[p][2]:
            s_line_add(p, 1)
        else:
            s_rest(p, 1)
        go(s_hop(p, groups[g][-1]))

    def s_z(p):
        s_rest(p, 1 if routes[p][2] else 0)
        go(s_line(p, 0))

    def s_z1(p):
        s_line_add(p, 0)
        go(s_line(p, 1))

    def s_out(p):
        if routes[p][2]:
            for s in reversed(range(1, half)):
                s_added(p, s)
                go(s_hop(p, s - 1))
            received(s_hop(p, 0))
            other = r.rh[p, 0, :, :lanes]
        else:
            received(s_line(p, 1))
            other = r.rz[p, 2, 0]
        own_place(p)[...] = part(p, at.d, columns(at.t))[...].astype(F32) + other.astype(F32)
        own_move(p).start()

    def own_place(p):
        return r.unit1.at[pl.ds(p // SPLIT * rows, rows), pl.ds(p % SPLIT * lanes, lanes)]

    def own_move(p):
        return pltpu.make_async_copy(own_place(p), own_out.at[p], r.osem.at[p])

    def s_sent():
        for p in range(pieces):
            sent(s_core(p) + s_line(p, 0) + s_line(p, 1))
            for s in range(hops):
                sent(s_hop(p, s))


    def token_block(t):
        return span(t * share, share)

    def exchange(n, k, src, dst):
        return copy(src(peers[k]), dst, r.us.at[n, k], r.ur.at[n, k], at.at(t=peers[k]))

    def keep(n, src, dst):
        return pltpu.make_async_copy(src(at.t), dst, r.lsem.at[n])

    def bias_move(k=None):
        args = (0, lambda t: r.bstage.at[0], r.bias.at[at.t])
        return keep(*args) if k is None else exchange(args[0], k, *args[1:])

    def cot_move(k=None):
        args = (1, lambda t: cot.at[t], r.cot.at[token_block(at.t)])
        return keep(*args) if k is None else exchange(args[0], k, *args[1:])

    def out_move(k=None):
        args = (2, lambda t: r.out.at[token_block(t)], layer_out.at[at.t])
        return keep(*args) if k is None else exchange(args[0], k, *args[1:])

    def gx_move(k=None):
        args = (3, lambda t: r.n1.at[token_block(t)], gx_out.at[at.t])
        return keep(*args) if k is None else exchange(args[0], k, *args[1:])

    every = (None, 0, 1, 2)

    links = [1] + at.links
    base = len(links)

    def v_pack():
        for k in range(6):
            r.vec[k:k + 1, :] = jnp.sum(r.sums[k], axis=0, keepdims=True)
        r.vec[6:7, :] = jnp.sum(r.qsum[...].T, axis=0, keepdims=True)
        r.vec[7:8, :] = jnp.sum(r.vsum[...].T, axis=0, keepdims=True)
        for k in range(SPLIT):
            row = jnp.sum(r.isum[k], axis=0, keepdims=True)
            for t in range(tp):
                r.vec[8 + t:9 + t, k * lanes:(k + 1) * lanes] = row[:, t * lanes:(t + 1) * lanes]
        r.vec[8 + tp:, :] = jnp.zeros((8 - tp, D), F32)

    def v_hop(i):
        return copy(r.vec, r.rv.at[i], r.vs.at[i], r.vr.at[i], at.at(d=flip(at.d, links[i])))

    def v_end(i):
        v_hop(i).wait()
        r.vec[...] = r.vec[...] + r.rv[i]

    def v_line():
        return [copy(r.vec, r.rv.at[base + at.t], r.vs.at[base + k], r.vr.at[base + k], at.at(t=peers[k])) for k in range(tp - 1)]

    def v_out():
        done(v_line())
        total = r.rv[base]
        for k in range(1, tp):
            total += r.rv[base + k]
        r.vec[...] = total
        vec_move().start()

    def vec_move():
        return pltpu.make_async_copy(r.vec, vec_out, r.osem.at[pieces])

    def pair(n):
        return range(n % 2 * (tp // 2), (n % 2 + 1) * (tp // 2))

    def start():
        fetches = [pltpu.make_async_copy(src, dst, r.fsem.at[n]) for n, (src, dst) in enumerate(zip(ins[3:], local))]
        fetches.append(pltpu.make_async_copy(inputs.at[at.t], r.x, r.fsem.at[len(local)]))
        go(fetches)
        at.greet()
        done(fetches[:9])
        place_weights()
        at.meet()
        for p in range(pieces):
            a_first(p)
        go([bias_move(k) for k in every])
        done(fetches[9:])
        r.out_bias, r.gain1, r.shift1, r.outer_bias, r.gain2, r.shift2 = [v[...].reshape(1, D) for v in vectors_in]
        L.prepare()

    def project_in(k):
        if k == 0:
            done([bias_move(n) for n in every])
        L.project_in(k)

    def vectors(i):
        for k in range(i, i + 1 if i < 3 else base + 1):
            if k == 0:
                v_pack()
            else:
                v_end(k - 1)
            if k < base:
                v_hop(k).start()
            else:
                go(v_line())
                r.rv[base + at.t] = r.vec[...]

    def leave():
        a_sent()
        go([out_move(k) for k in every])

    tasks = {
        "astart": a_start, "az1": a_z1, "az2": a_z2, "ahop": a_group, "aready": a_ready,
        "proj": project_in,
        "attend": lambda n: count_loop(pair(n)[0], pair(n)[-1] + 1, partial(L.attend, n // 2)),
        "project": L.project_out, "norm1": L.norm1,
        "inner": lambda p: L.inner(p - 3),
        "outer": lambda p: L.outer(p - 6),
        "cots": lambda: go([cot_move(k) for k in every]), "cotr": lambda: done([cot_move(k) for k in every]),
        "norm2": L.norm2, "outs": leave, "outr": lambda: done([out_move(k) for k in every]),
        "grad": lambda p: (L.mixed_grad, L.inner_grad, L.outer_grad)[p // 3](p % 3),
        "iback": lambda p: L.inner_back(p - 6),
        "back": lambda p: L.back(p - 3),
        "norm1b": L.norm1_back, "outg": L.out_back,
        "attback": lambda n: L.attend_back(n // 2, pair(n)),
        "gx": L.input_grad,
        "gxs": lambda k: go([gx_move(k)] + ([gx_move()] if k == 0 else [])),
        "gxw": lambda k: gx_move(k).wait_recv(),
        "gxr": lambda: (sent([gx_move(k) for k in every[1:]]), gx_move().wait()),
        "score": lambda p: go(s_core(p)), "shop": s_group, "sz": s_z, "sz1": s_z1, "sout": s_out,
        "vec": vectors, "vout": v_out,
    }
    start()
    for name, *args in order:
        tasks[name](*args)
    s_sent()
    done([own_move(p) for p in range(pieces)])
    done([vec_move()])


def scratch_list(dp, tp):
    VM, dma = pltpu.VMEM, pltpu.SemaphoreType.DMA
    lanes, wide, seq = FF // tp // SPLIT, FF // SPLIT, SEQ
    rows = D // dp
    pieces, blocks, nv, heads = 3 * SPLIT, dp // 2, dp.bit_length() - 1 + tp, D // HEAD
    most = 1 << ((dp.bit_length() - 2) // 2)
    return [
        ("w", VM((pieces, D, wide), BF)), ("dc", VM((SPLIT, D, wide), BF)), ("stage", VM((pieces, rows, lanes), BF)),
        ("x", VM((seq, D), BF)), ("xt", VM((D, seq), BF)), ("cot", VM((seq, D), BF)), ("gt", VM((D, seq), BF)), ("n1", VM((seq, D), BF)), ("n1t", VM((D, seq), BF)),
        ("bstage", VM((1, 1, 2 * D), F32)), ("line", VM((1, wide), F32)), ("bias", VM((tp, 1, 2 * D), F32)),
        ("qkv", VM((SPLIT, wide, seq), BF)), ("attt", VM((wide, seq), BF)), ("att", VM((seq, wide), BF)),
        ("pt", VM((heads, seq, seq), BF)), ("linv", VM((heads, 1, seq), F32)),
        ("unit1", VM((seq, D), F32)), ("inv1", VM((seq, 128), F32)), ("acc", VM((seq, D), F32)),
        ("act", VM((SPLIT, seq, wide), BF)), ("slope", VM((SPLIT, seq, wide), BF)),
        ("sums", VM((6, 8, D), F32)), ("isum", VM((SPLIT, 8, wide), F32)), ("qsum", VM((D, 128), F32)), ("vsum", VM((D, 128), F32)),
        ("rc", VM((pieces, blocks, rows, wide), BF)), ("rh", VM((pieces, blocks - 1, rows, wide), BF)),
        ("rz", VM((pieces, 3, most, rows, lanes), BF)),
        ("vec", VM((16, D), F32)), ("rv", VM((nv, 16, D), F32)),
        ("lsem", dma((4,))), ("fsem", dma((16,))), ("osem", dma((pieces + 1,))), ("zs", dma((pieces, 3, most))), ("zr", dma((pieces, 3, most))), ("hs", dma((pieces, blocks - 1))), ("hr", dma((pieces, blocks - 1))),
        ("cs", dma((pieces, blocks))), ("cr", dma((pieces, blocks))), ("scs", dma((pieces, blocks))), ("scr", dma((pieces, blocks))),
        ("shs", dma((pieces, blocks - 1))), ("shr", dma((pieces, blocks - 1))), ("szs", dma((pieces, 3, most))), ("szr", dma((pieces, 3, most))),
        ("us", dma((4, tp - 1))), ("ur", dma((4, tp - 1))), ("vs", dma((nv,))), ("vr", dma((nv,))),
    ]


def layer_call(dp, tp, operands, share):
    A, M = pl.BlockSpec(memory_space=pl.ANY), pl.BlockSpec(memory_space=pltpu.SMEM)
    S = jax.ShapeDtypeStruct
    half = (dp.bit_length() - 2) // 2
    return pl.pallas_call(
        partial(layer_kernel, dp, tp, ORDER, [(half * a, direct, half * b) for a, direct, b in ROUTES], len(operands), 4),
        out_shape=(S((3 * SPLIT, D // dp, FF // tp // SPLIT), F32), S((16, D), F32), S((tp, share, D), BF), S((tp, share, D), BF)),
        in_specs=[M] + [A] * (len(operands) - 1),
        out_specs=(A,) * 4,
        scratch_shapes=[s for _, s in scratch_list(dp, tp)] + [pltpu.VMEM(v.shape, v.dtype) for v in operands[3:]],
        compiler_params=pltpu.CompilerParams(collective_id=0, has_side_effects=True, vmem_limit_bytes=67043328),
        name="layer",
    )(*operands)


def results_kernel(tp, own, vec, out, gx, o_out, o_gx, g_query, g_key, g_value, b_query, b_value, g_out, v_out, v_gain1, v_shift1, g_inner, b_inner,
                   g_outer, v_outer, v_gain2, v_shift2):
    t = lax.axis_index("tensor")
    head = D // tp
    o_out[...] = out[...]
    for s in range(tp):
        o_gx[s] = gx[s].astype(F32)
    for ref, places in ((g_query, QUERY), (g_key, KEY), (g_value, VALUE)):
        ref[...] = jnp.concatenate([own[k, :, n * HEAD:(n + 1) * HEAD] for k, n in places], axis=1)
    g_out[...] = own[0, :, :head].T
    for k in range(SPLIT):
        g_inner[:, k * 256:(k + 1) * 256] = own[3 + k]
        g_outer[:, k * 256:(k + 1) * 256] = own[6 + k]
    for ref, row in ((v_out, 0), (v_gain1, 1), (v_shift1, 2), (v_outer, 3), (v_gain2, 4), (v_shift2, 5)):
        ref[...] = vec[row:row + 1, :].reshape(D)
    for k in range(tp):
        @pl.when(t == k)
        def _():
            b_query[...] = vec[6:7, k * head:(k + 1) * head].reshape(head)
            b_value[...] = vec[7:8, k * head:(k + 1) * head].reshape(head)
            b_inner[...] = vec[8 + k:9 + k, :].reshape(D)


def shards(dp, tp, inputs, lengths, w_query, w_key, w_value, query_bias, value_bias, w_out, out_bias, norm1_gain, norm1_shift,
           w_inner, inner_bias, w_outer, outer_bias, norm2_gain, norm2_shift, cotangent):
    operands = (lengths, inputs, cotangent, w_query, w_key, w_value, w_out, w_inner, w_outer.T, query_bias, value_bias, inner_bias,
                out_bias, norm1_gain, norm1_shift, outer_bias, norm2_gain, norm2_shift)
    share = cotangent.shape[1]
    own, vec, out, grad_in = layer_call(dp, tp, operands, share)
    like = lambda v: jax.ShapeDtypeStruct(v.shape, F32)
    results = pl.pallas_call(
        partial(results_kernel, tp),
        out_shape=(
            jax.ShapeDtypeStruct(cotangent.shape, BF), like(cotangent), like(w_query), like(w_key), like(w_value), like(query_bias), like(value_bias),
            like(w_out), like(out_bias), like(norm1_gain), like(norm1_shift), like(w_inner), like(inner_bias), like(w_outer.T), like(outer_bias),
            like(norm2_gain), like(norm2_shift),
        ),
        name="results",
    )(own, vec, out, grad_in)
    return results[:13] + (results[13].T,) + results[14:]


def solution(mesh):
    dp, tp = mesh.shape["dp"], mesh.shape["tensor"]
    rows, cols = P("dp", "tensor"), P("tensor", "dp")
    tokens = P("dp", "tensor", None)
    tensor, whole = P("tensor"), P()
    return jax.shard_map(
        partial(shards, dp, tp),
        mesh=mesh,
        in_specs=(P("dp", None, None), P("dp"), rows, rows, rows, tensor, tensor, cols, whole, whole, whole, rows, tensor, cols,
                  whole, whole, whole, tokens),
        out_specs=(tokens, tokens, rows, rows, rows, tensor, tensor, cols, whole, whole, whole, rows, tensor, cols, whole, whole, whole),
        check_vma=False,
    )
```

```python
from functools import partial
from types import SimpleNamespace

import jax
import jax.numpy as jnp
from jax import lax
from jax.experimental import pallas as pl
from jax.experimental.pallas import tpu as pltpu
from jax.sharding import PartitionSpec as P

D = 768
HEAD = 64
FF = 3072
SPLIT = 3
SEQ = 512
BF = jnp.bfloat16
F32 = jnp.float32

ROUTES = ((0, 0, 0), (0, 0, 0), (0, 0, 0), (0, 0, 0), (0, 0, 0), (0, 0, 0), (1, 0, 0), (0, 0, 0), (1, 0, 0))
ORDER = (
    ("astart", 0), ("astart", 1), ("az1", 0), ("astart", 2), ("az1", 1), ("astart", 3), ("az2", 0), ("az1", 2), ("astart", 4), ("az2", 1),
    ("ahop", 0, 0), ("az1", 3), ("astart", 5), ("az2", 2), ("ahop", 1, 0), ("az1", 4), ("astart", 6), ("az2", 3), ("az1", 5), ("astart", 7),
    ("ahop", 2, 0), ("ahop", 0, 1), ("az2", 4), ("aready", 0), ("proj", 0), ("ahop", 3, 0), ("az1", 6), ("astart", 8), ("az2", 5), ("ahop", 4, 0),
    ("az1", 7), ("ahop", 1, 1), ("aready", 1), ("proj", 1), ("attend", 0), ("ahop", 5, 0), ("attend", 1), ("az2", 6), ("az1", 8), ("ahop", 2, 1),
    ("az2", 7), ("cots",), ("aready", 2), ("proj", 2), ("attend", 2), ("attend", 3), ("ahop", 3, 1), ("attend", 4), ("attend", 5), ("ahop", 7, 0),
    ("project",), ("norm1",), ("az2", 8), ("aready", 3), ("inner", 3), ("ahop", 4, 1), ("aready", 4), ("inner", 4), ("ahop", 5, 1), ("aready", 5),
    ("inner", 5), ("ahop", 6, 1), ("aready", 6), ("outer", 6), ("ahop", 7, 1), ("aready", 7), ("outer", 7), ("ahop", 8, 1), ("cotr",), ("aready", 8),
    ("outer", 8), ("norm2",), ("outs",), ("grad", 6), ("score", 6), ("grad", 7), ("score", 7), ("grad", 8), ("score", 8), ("iback", 6),
    ("shop", 6, 1), ("iback", 7), ("shop", 7, 1), ("iback", 8), ("back", 3), ("back", 4), ("back", 5), ("norm1b",), ("shop", 6, 0), ("shop", 8, 1),
    ("outg",), ("attback", 0), ("attback", 1), ("shop", 7, 0), ("grad", 3), ("score", 3), ("sz", 6), ("grad", 4), ("score", 4), ("grad", 5),
    ("score", 5), ("shop", 3, 1), ("grad", 0), ("score", 0), ("shop", 8, 0), ("shop", 4, 1), ("sz", 7), ("attback", 2), ("attback", 3), ("grad", 1),
    ("score", 1), ("attback", 4), ("shop", 3, 0), ("shop", 5, 1), ("sz1", 6), ("sz1", 7), ("sz", 8), ("attback", 5), ("vec", 0), ("gx",),
    ("shop", 4, 0), ("shop", 0, 1), ("sout", 6), ("sz", 3), ("gxs", 0), ("gxs", 1), ("grad", 2), ("score", 2), ("vec", 1), ("sout", 7), ("outr",),
    ("sz1", 8), ("shop", 5, 0), ("shop", 1, 1), ("sz", 4), ("sz1", 3), ("sz", 5), ("shop", 0, 0), ("shop", 2, 1), ("gxw", 0), ("gxs", 2), ("sz", 0),
    ("shop", 1, 0), ("sout", 8), ("sz1", 4), ("sout", 3), ("sz", 1), ("shop", 2, 0), ("vec", 2), ("sz1", 5), ("sz", 2), ("vec", 3), ("gxw", 1),
    ("gxw", 2), ("gxr",), ("sz1", 0), ("sout", 4), ("sz1", 1), ("sout", 5), ("sz1", 2), ("sout", 0), ("sout", 1), ("sout", 2), ("vout",),
)


def flip(index, bit):
    return index + bit * (1 - 2 * ((index // bit) % 2))


class Place:
    def __init__(self, dp, tp):
        self.dp, self.tp = dp, tp
        self.d = lax.axis_index("dp")
        self.t = lax.axis_index("tensor")
        self.c = self.d % 2
        count = dp.bit_length() - 1
        links = [1 << k for k in range(1, count)]
        half = len(links) // 2
        self.order0 = links
        self.order1 = links[half:] + links[:half]
        self.hops = len(links)
        self.links = links

    def mix(self, zero, one):
        return zero * (1 - self.c) + one * self.c

    def across(self, hop):
        return self.mix(flip(self.d, self.order0[hop]), flip(self.d, self.order1[hop]))

    def subset(self, hop, j, crossed):
        zero, one = self.d, self.d
        if crossed:
            zero, one = flip(zero, self.order0[hop]), flip(one, self.order1[hop])
        for k in range(hop):
            if (j >> k) & 1:
                zero, one = flip(zero, self.order0[k]), flip(one, self.order1[k])
        return self.mix(zero, one)

    def at(self, d=None, t=None):
        return {"dp": self.d if d is None else d, "tensor": self.t if t is None else t}

    def neighbours(self):
        return [self.at(t=(self.t + k) % self.tp) for k in range(1, self.tp)] + [self.at(d=flip(self.d, bit)) for bit in [1] + self.links]

    def greet(self):
        for device in self.neighbours():
            pl.semaphore_signal(pltpu.get_barrier_semaphore(), 1, device_id=device, device_id_type=pl.DeviceIdType.MESH)

    def meet(self):
        pl.semaphore_wait(pltpu.get_barrier_semaphore(), len(self.neighbours()))


EPS = 1e-06
NORM_ROWS = 256


def dot(a, b):
    return jnp.dot(a, b, preferred_element_type=F32)


def dot_nt(a, b):
    return lax.dot_general(a, b, (((1,), (1,)), ((), ())), preferred_element_type=F32)


def dot_tn(a, b):
    return lax.dot_general(a, b, (((0,), (0,)), ((), ())), preferred_element_type=F32)


def mean(v):
    return jnp.sum(v, axis=-1, keepdims=True) * (1.0 / D)


def count_loop(first, last, body):
    def run(i, carry):
        body(i)
        return carry

    lax.fori_loop(first, last, run, 0)


def span(start, size, step=None):
    return pl.ds(pl.multiple_of(start, step or size), size)


QUERY, KEY, VALUE = ((0, 3), (1, 2), (2, 1)), ((1, 0), (1, 3), (2, 2)), ((1, 1), (2, 0), (2, 3))


class Layer:
    def __init__(self, r, tp):
        self.r, self.tp = r, tp
        self.seq = r.x.shape[0]
        self.head = D // tp
        self.per = self.head // HEAD
        self.wide = r.w.shape[2]
        self.lanes = self.wide // tp

    def bias(self, k):
        return jnp.concatenate([self.r.bias[t, :, pl.ds(k * self.lanes, self.lanes)] for t in range(self.tp)], axis=1)

    def pairs(self, body):
        step = 2 * self.lanes
        count_loop(0, self.wide // step, lambda n: body(span(n * step, step)))

    def place(self, where, t):
        k, chunk = where
        return k, span(t * self.lanes + chunk * HEAD, HEAD)

    def prepare(self):
        r = self.r
        r.xt[...] = r.x[...].T
        for t in range(self.tp):
            r.qkv[0, pl.ds(t * self.lanes, self.head), :] = jnp.zeros((self.head, self.seq), BF)
            r.attt[pl.ds(t * self.lanes + self.head, HEAD), :] = jnp.zeros((HEAD, self.seq), BF)

    def project_in(self, k):
        r = self.r
        r.line[...] = self.bias(k)
        chunk = lax.broadcasted_iota(jnp.int32, (1, 2 * self.lanes), 1) % self.lanes // HEAD
        scale = jnp.where(chunk == QUERY[k][1], HEAD ** -0.5, 1.0)

        def body(cols):
            rows = ((dot(r.x[...], r.w[k, :, cols]) + r.line[:, cols]) * scale).astype(BF).T
            if k:
                r.qkv[k, cols, :] = rows
            else:
                for n in range(2):
                    start = n * self.lanes + self.head
                    r.qkv[0, span(cols.start + start, HEAD), :] = rows[start:start + HEAD]

        self.pairs(body)

    def attend(self, i, t):
        r = self.r
        qt, kt, vt = [r.qkv[self.place(kind[i], t)] for kind in (QUERY, KEY, VALUE)]
        key = lax.broadcasted_iota(jnp.int32, (self.seq, 1), 0)
        scores = jnp.where(key < r.length, dot_tn(kt, qt), -1000000000.0)
        expons = jnp.exp(scores - jnp.max(scores, axis=0, keepdims=True))
        inverse = 1.0 / jnp.sum(expons, axis=0, keepdims=True)
        expons = expons.astype(BF)
        r.pt[t * self.per + i] = expons
        r.linv[t * self.per + i] = inverse
        r.attt[self.place((0, i), t)[1], :] = (dot(vt, expons) * inverse).astype(BF)

    def project_out(self):
        r = self.r
        r.att[...] = r.attt[...].T
        for n in range(D // 256):
            cols = pl.ds(n * 256, 256)
            r.acc[:, cols] = dot_nt(r.att[...], r.w[0, cols, :])

    def norm1(self):
        r = self.r

        def body(i):
            rows = span(i * NORM_ROWS, NORM_ROWS)
            res = r.x[rows, :].astype(F32) + r.acc[rows, :] + r.out_bias
            centred = res - mean(res)
            inv = lax.rsqrt(mean(centred * centred) + EPS)
            unit = centred * inv
            r.unit1[rows, :] = unit
            r.inv1[rows, :] = jnp.broadcast_to(inv, (inv.shape[0], 128))
            r.n1[rows, :] = (unit * r.gain1 + r.shift1).astype(BF)

        count_loop(0, self.seq // NORM_ROWS, body)
        r.n1t[...] = r.n1[...].T

    def inner(self, k):
        r = self.r
        r.line[...] = self.bias(3 + k)

        def body(cols):
            u = dot(r.n1[...], r.w[3 + k, :, cols]) + r.line[:, cols]
            half = 0.5 + 0.5 * lax.erf(u * (2.0 ** -0.5))
            r.act[k, :, cols] = (u * half).astype(BF)
            r.slope[k, :, cols] = (half + u * jnp.exp(-0.5 * u * u) * (2 * jnp.pi) ** -0.5).astype(BF)

        self.pairs(body)

    def outer(self, k):
        r = self.r
        for n in range(D // 256):
            cols = pl.ds(n * 256, 256)
            part = dot_nt(r.act[k], r.w[6 + k, cols, :])
            if k == 0:
                r.acc[:, cols] = part
            else:
                r.acc[:, cols] += part

    def norm2(self):
        r = self.r
        r.sums[...] = jnp.zeros_like(r.sums)

        def body(i):
            rows = span(i * NORM_ROWS, NORM_ROWS)
            res = r.unit1[rows, :] * r.gain1 + r.shift1 + r.acc[rows, :] + r.outer_bias
            centred = res - mean(res)
            inv = lax.rsqrt(mean(centred * centred) + EPS)
            unit = centred * inv
            r.out[rows, :] = (unit * r.gain2 + r.shift2).astype(BF)
            grad = self.norm_back(r.cot[rows, :].astype(F32), unit, inv, r.gain2, 3)
            r.acc[rows, :] = grad
            r.g[rows, :] = grad.astype(BF)

        count_loop(0, self.seq // NORM_ROWS, body)
        r.gt[...] = r.g[...].T

    def norm_back(self, up, unit, inv, gain, slot):
        r = self.r
        scaled = up * gain
        grad = inv * (scaled - mean(scaled) - unit * mean(scaled * unit))

        def total(v):
            return jnp.sum(v.reshape(-1, 8, D), axis=0)

        r.sums[slot] += total(grad)
        r.sums[slot + 1] += total(up * unit)
        r.sums[slot + 2] += total(up)
        return grad

    def outer_grad(self, k):
        r = self.r
        r.dc[k] = dot(r.gt[...], r.act[k]).astype(BF)

    def inner_back(self, k):
        r = self.r

        def body(cols):
            grad = dot(r.g[...], r.w[6 + k, :, cols]) * r.slope[k, :, cols].astype(F32)
            r.isum[k, :, cols] = jnp.sum(grad.reshape(-1, 8, cols.size), axis=0)
            r.slope[k, :, cols] = grad.astype(BF)

        self.pairs(body)

    def inner_grad(self, k):
        r = self.r

        def body(cols):
            r.w[6 + k, :, cols] = dot(r.n1t[...], r.slope[k, :, cols]).astype(BF)

        self.pairs(body)

    def back(self, k):
        r = self.r
        for n in range(D // 256):
            cols = pl.ds(n * 256, 256)
            r.acc[:, cols] += dot_nt(r.slope[k], r.w[3 + k, cols, :])

    def norm1_back(self):
        r = self.r

        def body(i):
            rows = span(i * NORM_ROWS, NORM_ROWS)
            grad = self.norm_back(r.acc[rows, :], r.unit1[rows, :], r.inv1[rows, :1], r.gain1, 0)
            r.acc[rows, :] = grad
            r.g[rows, :] = grad.astype(BF)

        count_loop(0, self.seq // NORM_ROWS, body)
        r.gt[...] = r.g[...].T

    def out_back(self):
        r = self.r
        r.attt[...] = dot(r.g[...], r.w[0]).astype(BF).T

    def attend_back(self, i, ts):
        r = self.r
        loaded = []
        for t in ts:
            inverse = r.linv[t * self.per + i]
            gat = (r.attt[self.place((0, i), t)[1], :].astype(F32) * inverse).astype(BF)
            loaded.append([r.qkv[self.place(kind[i], t)] for kind in (QUERY, KEY, VALUE)] + [inverse, gat])
        found = []
        for t, (qt, kt, vt, inverse, gat) in zip(ts, loaded):
            expons = r.pt[t * self.per + i]
            gp = dot_tn(vt, gat)
            wide = expons.astype(F32)
            delta = jnp.sum(wide * gp, axis=0, keepdims=True) * inverse
            gs = (wide * (gp - delta)).astype(BF)
            found.append((dot(kt, gs) * HEAD ** -0.5, dot_nt(qt, gs), dot_nt(gat, expons)))

        def fold(v):
            return sum(v[:, n:n + 128] for n in range(128, self.seq, 128)) + v[:, :128]

        for t, grads in zip(ts, found):
            for kind, grad in zip((QUERY, KEY, VALUE), grads):
                r.qkv[self.place(kind[i], t)] = grad.astype(BF)
            rows = pl.ds((t * self.per + i) * HEAD, HEAD)
            r.qsum[rows, :] = fold(grads[0])
            r.vsum[rows, :] = fold(grads[2])

    def mixed_grad(self, k):
        r = self.r
        grad = dot_nt(r.xt[...], r.qkv[k])
        if k == 0:
            grad += dot(r.gt[...], r.att[...])
        r.w[3 + k] = grad.astype(BF)

    def input_grad(self):
        r = self.r
        for n in range(self.seq // 256):
            tokens = pl.ds(n * 256, 256)
            total = dot(r.w[0], r.qkv[0, :, tokens]) + dot(r.w[1], r.qkv[1, :, tokens]) + dot(r.w[2], r.qkv[2, :, tokens])
            r.n1[tokens, :] = (total.T + r.acc[tokens, :]).astype(BF)


def layer_kernel(dp, tp, order, routes, n_in, n_out, *refs):
    names = [n for n, _ in scratch_list(dp, tp)]
    ins, outs, rest = refs[:n_in], refs[n_in:n_in + n_out], refs[n_in + n_out:]
    r = SimpleNamespace(**dict(zip(names, rest)))
    lengths, inputs, cot = ins[:3]
    local = rest[len(names):]
    wq, wk, wv, wo, wi, wu, bq, bv, bi = local[:9]
    vectors_in = local[9:]
    own_out, vec_out, layer_out, gx_out = outs
    r.g, r.out = r.cot, r.x
    at = Place(dp, tp)
    pieces, rows, lanes = r.stage.shape
    share = cot.shape[1]
    hops, blocks = at.hops, dp // 2
    half = hops // 2
    groups = [range(half), range(half, hops)]
    r.length = lengths[at.t]
    L = Layer(r, tp)
    beside, two = flip(at.t, 1), flip(at.t, 2)
    peers = (beside, two, flip(two, 1))
    partner = at.at(d=flip(at.d, 1))

    def row_block(b):
        return span(b * rows, rows)

    def columns(t, count=1):
        return pl.ds(pl.multiple_of(t * (count * lanes), lanes), count * lanes)

    def copy(src, dst, ssem, rsem, device):
        return pltpu.make_async_remote_copy(src_ref=src, dst_ref=dst, send_sem=ssem, recv_sem=rsem, device_id=device, device_id_type=pl.DeviceIdType.MESH)

    def go(copies):
        for c in copies:
            c.start()

    def received(copies):
        for c in copies:
            c.wait_recv()

    def sent(copies):
        for c in copies:
            c.wait_send()

    def done(copies):
        for c in copies:
            c.wait()

    def weight(p, b, cols=None):
        return r.w.at[p, row_block(b)] if cols is None else r.w.at[p, row_block(b), cols]

    def place_weights():
        def cut(ref, i):
            return ref[:, i * HEAD:(i + 1) * HEAD]

        mixed = jnp.concatenate([wo[...].T, cut(wq, 0), cut(wk, 0), cut(wv, 0), cut(wq, 1), cut(wk, 1), cut(wv, 1), cut(wq, 2), cut(wk, 2), cut(wv, 2)], axis=1)
        outer = wu
        query, value = bq[...].reshape(1, -1), bv[...].reshape(1, -1)
        none = jnp.zeros((1, HEAD), F32)
        r.bstage[0, :, :D] = jnp.concatenate(
            [none] * 3 + [cut(query, 0), none, cut(value, 0), cut(query, 1), none, cut(value, 1), cut(query, 2), none, cut(value, 2)], axis=1
        )
        r.bstage[0, :, D:] = bi[...].reshape(1, -1)
        for p in range(pieces):
            k = p % SPLIT
            block = (mixed, wi, outer)[p // SPLIT][:, k * lanes:(k + 1) * lanes]
            r.stage[p] = block
            r.w[p, row_block(at.d), columns(at.t)] = block

    def a_hop(p, stage):
        out = []
        for j in range(1 << stage):
            b = at.subset(stage, j, False)
            n = (1 << stage) - 1 + j
            dst = weight(p, b, columns(at.t)) if stage < routes[p][0] else weight(p, b)
            src = r.stage.at[p] if stage == 0 and routes[p][0] else dst
            out.append(copy(src, dst, r.hs.at[p, n], r.hr.at[p, n], at.at(d=at.across(stage))))
        return out

    def a_core(p, fresh, base):
        return [copy(weight(p, b), weight(p, b), r.cs.at[p, base + n], r.cr.at[p, base + n], partner) for n, b in enumerate(fresh)]

    def a_core_z(p):
        return a_core(p, [at.subset(routes[p][0], j, False) for j in range(1 << routes[p][0])], 0)

    def a_core_hop(p, stage):
        return a_core(p, [at.subset(stage, j, True) for j in range(1 << stage)], 1 << stage)

    def a_line(p, step):
        if routes[p][1]:
            moves = [(at.t, peer) for peer in peers]
        else:
            moves = ([(at.t, two)], [(at.t, beside), (two, beside)])[step]
        out = []
        for n, (t, peer) in enumerate(moves):
            for j in range(1 << routes[p][0]):
                b = at.subset(routes[p][0], j, False)
                src = r.stage.at[p] if n == 0 and step == 0 and not routes[p][0] else weight(p, b, columns(t))
                k = n if routes[p][1] else step + n
                out.append(copy(src, weight(p, b, columns(t)), r.zs.at[p, k, j], r.zr.at[p, k, j], at.at(t=peer)))
        return out

    def a_first(p):
        if routes[p][0]:
            go(a_hop(p, 0))

    def a_start(p):
        if routes[p][0]:
            for s in groups[0]:
                received(a_hop(p, s))
                if s + 1 < half:
                    go(a_hop(p, s + 1))
        go(a_line(p, 0))

    def a_z1(p):
        received(a_line(p, 0))
        go(a_line(p, 1))

    def a_z2(p):
        received(a_line(p, 0 if routes[p][1] else 1))
        if routes[p][0] < hops:
            go(a_hop(p, routes[p][0]))
        go(a_core_z(p))

    def a_group(p, g):
        for s in groups[g]:
            received(a_hop(p, s))
            if s + 1 < hops:
                go(a_hop(p, s + 1))
            go(a_core_hop(p, s))

    def a_ready(p):
        received(a_core_z(p))
        for s in range(routes[p][0], hops):
            received(a_core_hop(p, s))

    def a_sent():
        for p in range(pieces):
            for s in range(hops):
                sent(a_hop(p, s))
                if s >= routes[p][0]:
                    sent(a_core_hop(p, s))
            sent(a_core_z(p) + a_line(p, 0))
            if not routes[p][1]:
                sent(a_line(p, 1))

    where = [r.w.at[3 + k] for k in range(3)] + [r.w.at[6 + k] for k in range(3)] + [r.dc.at[k] for k in range(3)]

    def part(p, b, cols=None):
        return where[p].at[row_block(b)] if cols is None else where[p].at[row_block(b), cols]

    def add(ref, other):
        ref[...] = ref[...] + other[...]

    def s_core(p):
        return [copy(part(p, 2 * j + (1 - at.c)), r.rc.at[p, j], r.scs.at[p, j], r.scr.at[p, j], partner) for j in range(blocks)]

    def s_hop(p, stage):
        first = (1 << stage) - 1
        out = []
        for j in range(1 << stage):
            src, dst = part(p, at.subset(stage, j, True)), r.rh.at[p, first + j]
            if stage < routes[p][2]:
                src, dst = part(p, at.subset(stage, j, True), columns(at.t)), r.rh.at[p, first + j, :, pl.ds(0, lanes)]
            out.append(copy(src, dst, r.shs.at[p, first + j], r.shr.at[p, first + j], at.at(d=at.across(stage))))
        return out

    def s_added(p, stage):
        received(s_hop(p, stage))
        for j in range(1 << stage):
            b, other = at.subset(stage, j, False), r.rh.at[p, (1 << stage) - 1 + j]
            if stage < routes[p][2]:
                add(part(p, b, columns(at.t)), other.at[:, pl.ds(0, lanes)])
            else:
                add(part(p, b), other)

    def s_rest(p, g):
        for s in reversed(groups[g]):
            s_added(p, s)
            if s != groups[g][0]:
                go(s_hop(p, s - 1))

    def s_line(p, step):
        moves = ([(beside, beside), (flip(two, 1), beside)], [(two, two)])[step]
        out = []
        for n, (t, peer) in enumerate(moves):
            for j in range(1 << routes[p][2]):
                src = part(p, at.subset(routes[p][2], j, False), columns(t))
                out.append(copy(src, r.rz.at[p, 2 * step + n, j], r.szs.at[p, 2 * step + n, j], r.szr.at[p, 2 * step + n, j], at.at(t=peer)))
        return out

    def s_line_add(p, step):
        received(s_line(p, step))
        for n, t in enumerate(((at.t, two), (at.t,))[step]):
            for j in range(1 << routes[p][2]):
                add(part(p, at.subset(routes[p][2], j, False), columns(t)), r.rz.at[p, 2 * step + n, j])

    def s_group(p, g):
        if g == 1:
            received(s_core(p))
            for j in range(blocks):
                add(part(p, 2 * j + at.c), r.rc.at[p, j])
        elif routes[p][2]:
            s_line_add(p, 1)
        else:
            s_rest(p, 1)
        go(s_hop(p, groups[g][-1]))

    def s_z(p):
        s_rest(p, 1 if routes[p][2] else 0)
        go(s_line(p, 0))

    def s_z1(p):
        s_line_add(p, 0)
        go(s_line(p, 1))

    def s_out(p):
        if routes[p][2]:
            for s in reversed(range(1, half)):
                s_added(p, s)
                go(s_hop(p, s - 1))
            received(s_hop(p, 0))
            other = r.rh[p, 0, :, :lanes]
        else:
            received(s_line(p, 1))
            other = r.rz[p, 2, 0]
        own_place(p)[...] = part(p, at.d, columns(at.t))[...].astype(F32) + other.astype(F32)
        own_move(p).start()

    def own_place(p):
        return r.unit1.at[pl.ds(p // SPLIT * rows, rows), pl.ds(p % SPLIT * lanes, lanes)]

    def own_move(p):
        return pltpu.make_async_copy(own_place(p), own_out.at[p], r.osem.at[p])

    def s_sent():
        for p in range(pieces):
            sent(s_core(p) + s_line(p, 0) + s_line(p, 1))
            for s in range(hops):
                sent(s_hop(p, s))


    def token_block(t):
        return span(t * share, share)

    def exchange(n, k, src, dst):
        return copy(src(peers[k]), dst, r.us.at[n, k], r.ur.at[n, k], at.at(t=peers[k]))

    def keep(n, src, dst):
        return pltpu.make_async_copy(src(at.t), dst, r.lsem.at[n])

    def bias_move(k=None):
        args = (0, lambda t: r.bstage.at[0], r.bias.at[at.t])
        return keep(*args) if k is None else exchange(args[0], k, *args[1:])

    def cot_move(k=None):
        args = (1, lambda t: cot.at[t], r.cot.at[token_block(at.t)])
        return keep(*args) if k is None else exchange(args[0], k, *args[1:])

    def out_move(k=None):
        args = (2, lambda t: r.out.at[token_block(t)], layer_out.at[at.t])
        return keep(*args) if k is None else exchange(args[0], k, *args[1:])

    def gx_move(k=None):
        args = (3, lambda t: r.n1.at[token_block(t)], gx_out.at[at.t])
        return keep(*args) if k is None else exchange(args[0], k, *args[1:])

    every = (None, 0, 1, 2)

    links = [1] + at.links
    base = len(links)

    def v_pack():
        for k in range(6):
            r.vec[k:k + 1, :] = jnp.sum(r.sums[k], axis=0, keepdims=True)
        r.vec[6:7, :] = jnp.sum(r.qsum[...].T, axis=0, keepdims=True)
        r.vec[7:8, :] = jnp.sum(r.vsum[...].T, axis=0, keepdims=True)
        for k in range(SPLIT):
            row = jnp.sum(r.isum[k], axis=0, keepdims=True)
            for t in range(tp):
                r.vec[8 + t:9 + t, k * lanes:(k + 1) * lanes] = row[:, t * lanes:(t + 1) * lanes]
        r.vec[8 + tp:, :] = jnp.zeros((8 - tp, D), F32)

    def v_hop(i):
        return copy(r.vec, r.rv.at[i], r.vs.at[i], r.vr.at[i], at.at(d=flip(at.d, links[i])))

    def v_end(i):
        v_hop(i).wait()
        r.vec[...] = r.vec[...] + r.rv[i]

    def v_line():
        return [copy(r.vec, r.rv.at[base + at.t], r.vs.at[base + k], r.vr.at[base + k], at.at(t=peers[k])) for k in range(tp - 1)]

    def v_out():
        done(v_line())
        total = r.rv[base]
        for k in range(1, tp):
            total += r.rv[base + k]
        r.vec[...] = total
        vec_move().start()

    def vec_move():
        return pltpu.make_async_copy(r.vec, vec_out, r.osem.at[pieces])

    def pair(n):
        return range(n % 2 * (tp // 2), (n % 2 + 1) * (tp // 2))

    def start():
        fetches = [pltpu.make_async_copy(src, dst, r.fsem.at[n]) for n, (src, dst) in enumerate(zip(ins[3:], local))]
        fetches.append(pltpu.make_async_copy(inputs.at[at.t], r.x, r.fsem.at[len(local)]))
        go(fetches)
        at.greet()
        done(fetches[:9])
        place_weights()
        at.meet()
        for p in range(pieces):
            a_first(p)
        go([bias_move(k) for k in every])
        done(fetches[9:])
        r.out_bias, r.gain1, r.shift1, r.outer_bias, r.gain2, r.shift2 = [v[...].reshape(1, D) for v in vectors_in]
        L.prepare()

    def project_in(k):
        if k == 0:
            done([bias_move(n) for n in every])
        L.project_in(k)

    def vectors(i):
        for k in range(i, i + 1 if i < 3 else base + 1):
            if k == 0:
                v_pack()
            else:
                v_end(k - 1)
            if k < base:
                v_hop(k).start()
            else:
                go(v_line())
                r.rv[base + at.t] = r.vec[...]

    def leave():
        a_sent()
        go([out_move(k) for k in every])

    tasks = {
        "astart": a_start, "az1": a_z1, "az2": a_z2, "ahop": a_group, "aready": a_ready,
        "proj": project_in,
        "attend": lambda n: count_loop(pair(n)[0], pair(n)[-1] + 1, partial(L.attend, n // 2)),
        "project": L.project_out, "norm1": L.norm1,
        "inner": lambda p: L.inner(p - 3),
        "outer": lambda p: L.outer(p - 6),
        "cots": lambda: go([cot_move(k) for k in every]), "cotr": lambda: done([cot_move(k) for k in every]),
        "norm2": L.norm2, "outs": leave, "outr": lambda: done([out_move(k) for k in every]),
        "grad": lambda p: (L.mixed_grad, L.inner_grad, L.outer_grad)[p // 3](p % 3),
        "iback": lambda p: L.inner_back(p - 6),
        "back": lambda p: L.back(p - 3),
        "norm1b": L.norm1_back, "outg": L.out_back,
        "attback": lambda n: L.attend_back(n // 2, pair(n)),
        "gx": L.input_grad,
        "gxs": lambda k: go([gx_move(k)] + ([gx_move()] if k == 0 else [])),
        "gxw": lambda k: gx_move(k).wait_recv(),
        "gxr": lambda: (sent([gx_move(k) for k in every[1:]]), gx_move().wait()),
        "score": lambda p: go(s_core(p)), "shop": s_group, "sz": s_z, "sz1": s_z1, "sout": s_out,
        "vec": vectors, "vout": v_out,
    }
    start()
    for name, *args in order:
        tasks[name](*args)
    s_sent()
    done([own_move(p) for p in range(pieces)])
    done([vec_move()])


def scratch_list(dp, tp):
    VM, dma = pltpu.VMEM, pltpu.SemaphoreType.DMA
    lanes, wide, seq = FF // tp // SPLIT, FF // SPLIT, SEQ
    rows = D // dp
    pieces, blocks, nv, heads = 3 * SPLIT, dp // 2, dp.bit_length() - 1 + tp, D // HEAD
    most = 1 << ((dp.bit_length() - 2) // 2)
    return [
        ("w", VM((pieces, D, wide), BF)), ("dc", VM((SPLIT, D, wide), BF)), ("stage", VM((pieces, rows, lanes), BF)),
        ("x", VM((seq, D), BF)), ("xt", VM((D, seq), BF)), ("cot", VM((seq, D), BF)), ("gt", VM((D, seq), BF)), ("n1", VM((seq, D), BF)), ("n1t", VM((D, seq), BF)),
        ("bstage", VM((1, 1, 2 * D), F32)), ("line", VM((1, wide), F32)), ("bias", VM((tp, 1, 2 * D), F32)),
        ("qkv", VM((SPLIT, wide, seq), BF)), ("attt", VM((wide, seq), BF)), ("att", VM((seq, wide), BF)),
        ("pt", VM((heads, seq, seq), BF)), ("linv", VM((heads, 1, seq), F32)),
        ("unit1", VM((seq, D), F32)), ("inv1", VM((seq, 128), F32)), ("acc", VM((seq, D), F32)),
        ("act", VM((SPLIT, seq, wide), BF)), ("slope", VM((SPLIT, seq, wide), BF)),
        ("sums", VM((6, 8, D), F32)), ("isum", VM((SPLIT, 8, wide), F32)), ("qsum", VM((D, 128), F32)), ("vsum", VM((D, 128), F32)),
        ("rc", VM((pieces, blocks, rows, wide), BF)), ("rh", VM((pieces, blocks - 1, rows, wide), BF)),
        ("rz", VM((pieces, 3, most, rows, lanes), BF)),
        ("vec", VM((16, D), F32)), ("rv", VM((nv, 16, D), F32)),
        ("lsem", dma((4,))), ("fsem", dma((16,))), ("osem", dma((pieces + 1,))), ("zs", dma((pieces, 3, most))), ("zr", dma((pieces, 3, most))), ("hs", dma((pieces, blocks - 1))), ("hr", dma((pieces, blocks - 1))),
        ("cs", dma((pieces, blocks))), ("cr", dma((pieces, blocks))), ("scs", dma((pieces, blocks))), ("scr", dma((pieces, blocks))),
        ("shs", dma((pieces, blocks - 1))), ("shr", dma((pieces, blocks - 1))), ("szs", dma((pieces, 3, most))), ("szr", dma((pieces, 3, most))),
        ("us", dma((4, tp - 1))), ("ur", dma((4, tp - 1))), ("vs", dma((nv,))), ("vr", dma((nv,))),
    ]


def layer_call(dp, tp, operands, share):
    A, M = pl.BlockSpec(memory_space=pl.ANY), pl.BlockSpec(memory_space=pltpu.SMEM)
    S = jax.ShapeDtypeStruct
    half = (dp.bit_length() - 2) // 2
    return pl.pallas_call(
        partial(layer_kernel, dp, tp, ORDER, [(half * a, direct, half * b) for a, direct, b in ROUTES], len(operands), 4),
        out_shape=(S((3 * SPLIT, D // dp, FF // tp // SPLIT), F32), S((16, D), F32), S((tp, share, D), BF), S((tp, share, D), BF)),
        in_specs=[M] + [A] * (len(operands) - 1),
        out_specs=(A,) * 4,
        scratch_shapes=[s for _, s in scratch_list(dp, tp)] + [pltpu.VMEM(v.shape, v.dtype) for v in operands[3:]],
        compiler_params=pltpu.CompilerParams(collective_id=0, has_side_effects=True, vmem_limit_bytes=67043328),
        name="layer",
    )(*operands)


def results_kernel(tp, own, vec, out, gx, o_out, o_gx, g_query, g_key, g_value, b_query, b_value, g_out, v_out, v_gain1, v_shift1, g_inner, b_inner,
                   g_outer, v_outer, v_gain2, v_shift2):
    t = lax.axis_index("tensor")
    head = D // tp
    o_out[...] = out[...]
    for s in range(tp):
        o_gx[s] = gx[s].astype(F32)
    for ref, places in ((g_query, QUERY), (g_key, KEY), (g_value, VALUE)):
        ref[...] = jnp.concatenate([own[k, :, n * HEAD:(n + 1) * HEAD] for k, n in places], axis=1)
    g_out[...] = own[0, :, :head].T
    for k in range(SPLIT):
        g_inner[:, k * 256:(k + 1) * 256] = own[3 + k]
        g_outer[:, k * 256:(k + 1) * 256] = own[6 + k]
    for ref, row in ((v_out, 0), (v_gain1, 1), (v_shift1, 2), (v_outer, 3), (v_gain2, 4), (v_shift2, 5)):
        ref[...] = vec[row:row + 1, :].reshape(D)
    for k in range(tp):
        @pl.when(t == k)
        def _():
            b_query[...] = vec[6:7, k * head:(k + 1) * head].reshape(head)
            b_value[...] = vec[7:8, k * head:(k + 1) * head].reshape(head)
            b_inner[...] = vec[8 + k:9 + k, :].reshape(D)


def shards(dp, tp, inputs, lengths, w_query, w_key, w_value, query_bias, value_bias, w_out, out_bias, norm1_gain, norm1_shift,
           w_inner, inner_bias, w_outer, outer_bias, norm2_gain, norm2_shift, cotangent):
    operands = (lengths, inputs, cotangent, w_query, w_key, w_value, w_out, w_inner, w_outer.T, query_bias, value_bias, inner_bias,
                out_bias, norm1_gain, norm1_shift, outer_bias, norm2_gain, norm2_shift)
    share = cotangent.shape[1]
    own, vec, out, grad_in = layer_call(dp, tp, operands, share)
    like = lambda v: jax.ShapeDtypeStruct(v.shape, F32)
    results = pl.pallas_call(
        partial(results_kernel, tp),
        out_shape=(
            jax.ShapeDtypeStruct(cotangent.shape, BF), like(cotangent), like(w_query), like(w_key), like(w_value), like(query_bias), like(value_bias),
            like(w_out), like(out_bias), like(norm1_gain), like(norm1_shift), like(w_inner), like(inner_bias), like(w_outer.T), like(outer_bias),
            like(norm2_gain), like(norm2_shift),
        ),
        name="results",
    )(own, vec, out, grad_in)
    return results[:13] + (results[13].T,) + results[14:]


def solution(mesh):
    dp, tp = mesh.shape["dp"], mesh.shape["tensor"]
    rows, cols = P("dp", "tensor"), P("tensor", "dp")
    tokens = P("dp", "tensor", None)
    tensor, whole = P("tensor"), P()
    return jax.shard_map(
        partial(shards, dp, tp),
        mesh=mesh,
        in_specs=(P("dp", None, None), P("dp"), rows, rows, rows, tensor, tensor, cols, whole, whole, whole, rows, tensor, cols,
                  whole, whole, whole, tokens),
        out_specs=(tokens, tokens, rows, rows, rows, tensor, tensor, cols, whole, whole, whole, rows, tensor, cols, whole, whole, whole),
        check_vma=False,
    )
```
